256 devices in a mesh: zslab: 8 (over y_hi, x), xband: 32 (over y_lo, z, core).
Axes of the slice: x: 4, y: 4 (y_hi: 2, y_lo: 2; y = y_hi * 2 + y_lo), z: 8, core: 2. Of those that a mesh axis runs over, the one named last changes fastest.
Arguments:
- volume: float32 [32, 256, 512], P('xband', 'zslab'), may hold values from 0.2 to 1.8
- measured: float32 [32, 256, 512], P('xband', 'zslab'), may hold values from 6.4 to 57.6
- magnification: float32 [32, 32], P(None, 'xband'), may hold values from 1.25 to 2
- shift_y: int32 [32, 32], P(None, 'xband'), may hold values from -32 to 32
- shift_z: int32 [32, 32], P(None, 'xband'), may hold values from -4 to 4
Outputs:
- residual: float32 [32, 256, 512], P('xband', 'zslab')
- correction: float32 [32, 256, 512], P('xband', 'zslab')
The draws below stay inside these ranges and needn't reach their ends.
All inputs are finite; a program needn't handle non-finite values.
Results may differ from the reference program's by a relative error of at most 0.0003.
Values sent between devices are 32-bit elements; how exact they have to be, the bound alone decides.
A program may use at most 64 MiB of HBM per device.

```python
import math
import jax
import jax.numpy as jnp
from jax import lax

Y = 512
HALO = 4
SHIFT = 32
X = 32
Z = 256
ANGLES = 32


def plant(drawn, own_key, low, top_value):
    longest = drawn.shape.index(max(drawn.shape))
    spots = []
    for shift in (0, 1):
        where = [jax.random.randint(jax.random.fold_in(own_key, axis), (), 0, length) for axis, length in enumerate(drawn.shape)]
        where[longest] = (where[longest] + shift) % drawn.shape[longest]
        spots.append(tuple(where))
    return drawn.at[spots[0]].set(low).at[spots[1]].set(top_value)


def shard_levels(stream_key, shape, shards, smallest, top_value):
    level, own = 1.0, jax.random.fold_in(stream_key, 6)
    for dim, blocks in shards:
        heights = jnp.exp(jax.random.uniform(jax.random.fold_in(own, dim), (blocks,), jnp.float32, smallest / len(shards), top_value / len(shards)))
        level = level * jnp.repeat(heights, shape[dim] // blocks).reshape([-1 if axis == dim else 1 for axis in range(len(shape))])
    return level


def setup_inputs(seed: int = 0) -> dict:
    arg_keys = jax.random.split(jax.random.key(seed), 6)
    volume = jnp.clip(0.2 + 1.5999999 * jax.random.uniform(arg_keys[0], (X, Z, Y), jnp.float32) ** shard_levels(arg_keys[0], (X, Z, Y), ((0, 32), (1, 8)), -0.2, 0.2), 0.2, 1.8)
    measured = jnp.clip(6.4 + 51.199998 * jax.random.uniform(arg_keys[1], (ANGLES, Z, Y), jnp.float32) ** shard_levels(arg_keys[1], (ANGLES, Z, Y), ((0, 32), (1, 8)), -0.2, 0.2), 6.4, 57.6)
    magnification = jnp.clip(1.25 + 0.75 * jax.random.uniform(arg_keys[2], (ANGLES, X), jnp.float32) ** shard_levels(arg_keys[2], (ANGLES, X), ((1, 32),), -0.2, 0.2), 1.25, 2.0)
    shift_y = plant(jax.random.randint(arg_keys[3], (ANGLES, X), 0 - SHIFT, SHIFT + 1), jax.random.fold_in(arg_keys[3], 1), 0 - SHIFT, SHIFT).astype(jnp.int32)
    shift_z = plant(jax.random.randint(arg_keys[4], (ANGLES, X), 0 - HALO, HALO + 1), jax.random.fold_in(arg_keys[4], 1), 0 - HALO, HALO).astype(jnp.int32)
    return {"volume": volume, "measured": measured, "magnification": magnification, "shift_y": shift_y, "shift_z": shift_z}


def tap_tables(magnification, shift_y, index):
    columns = jnp.arange(Y, dtype=jnp.float32)
    centre = (Y - 1) / 2.0
    mags = lax.dynamic_index_in_dim(magnification, index, 1, keepdims=False)
    offsets = lax.dynamic_index_in_dim(shift_y, index, 1, keepdims=False).astype(jnp.float32)
    target = (columns[None, :] - centre) / mags[:, None] + centre + offsets[:, None]
    lower = jnp.floor(target)
    frac = target - lower
    return (lower.astype(jnp.int32), frac)

def reference(volume, measured, magnification, shift_y, shift_z):

    def forward_step(total, index):
        lower, frac = tap_tables(magnification, shift_y, index)
        slab = lax.dynamic_index_in_dim(volume, index, 0, keepdims=False)
        left = jnp.take(slab, lower, axis=1).transpose(1, 0, 2)
        right = jnp.take(slab, lower + 1, axis=1).transpose(1, 0, 2)
        image = (1.0 - frac)[:, None, :] * left + frac[:, None, :] * right
        padded = jnp.pad(image, ((0, 0), (HALO, HALO), (0, 0)))
        rowshift = lax.dynamic_index_in_dim(shift_z, index, 1, keepdims=False)
        placed = jax.vmap(lambda plane, offset: lax.dynamic_slice_in_dim(plane, (HALO - offset).astype(jnp.int32), Z, 0))(padded, rowshift)
        return (total + placed, None)
    proj, unused = lax.scan(forward_step, jnp.zeros((ANGLES, Z, Y), jnp.float32), jnp.arange(X, dtype=jnp.int32))
    gain = lax.optimization_barrier(jnp.sum(measured, axis=1)) / lax.optimization_barrier(jnp.sum(proj, axis=1))
    residual = (measured - gain[:, None, :] * proj) / X
    padded_res = jnp.pad(residual, ((0, 0), (HALO, HALO), (0, 0)))

    def backward_step(carry, index):
        lower, frac = tap_tables(magnification, shift_y, index)
        rowshift = lax.dynamic_index_in_dim(shift_z, index, 1, keepdims=False)
        rows = jax.vmap(lambda plane, offset: lax.dynamic_slice_in_dim(plane, (HALO + offset).astype(jnp.int32), Z, 0))(padded_res, rowshift)
        left_vals = ((1.0 - frac)[:, None, :] * rows).transpose(1, 0, 2).reshape(Z, ANGLES * Y)
        right_vals = (frac[:, None, :] * rows).transpose(1, 0, 2).reshape(Z, ANGLES * Y)
        plane = jnp.zeros((Z, Y), jnp.float32)
        plane = plane.at[:, lower.reshape(-1)].add(left_vals)
        plane = plane.at[:, (lower + 1).reshape(-1)].add(right_vals)
        return (carry, plane)
    unused2, planes = lax.scan(backward_step, jnp.zeros((), jnp.float32), jnp.arange(X, dtype=jnp.int32))
    correction = planes / math.sqrt(ANGLES)
    return (residual, correction)
```

```python
import math

import jax
import jax.numpy as jnp
from jax import lax
from jax.experimental import pallas as pl
from jax.experimental.pallas import tpu as pltpu
from jax.sharding import PartitionSpec as P

HALO = 4
TILES = 4
ROWS = 32
EXT = ROWS + 2 * HALO
SLABS = 8
RING = 8
BANDS = 32
CENTRE = 255.5
VOL_ROWS = TILES * ROWS + 8
RES_ROWS = TILES * EXT
VOL_A, VOL_B, VOL_ALL = (0, 64), (64, 72), (0, 136)
RES_A, RES_B, RES_ALL = (0, 80), (80, 80), (0, 160)
COPIES = 46
FORWARD_TILES = ((0, 1), (0, 1, 2), (1, 2, 3), (2, 3))
BACKWARD_TILES = ((0,), (0, 1), (0, 1), (1,))
MESH = pl.DeviceIdType.MESH


def take(x, index):
    return jnp.take_along_axis(x, index, axis=1, mode="promise_in_bounds")


def iota(axis):
    return lax.broadcasted_iota(jnp.int32, (8, 128), axis)


def project_block(blocks, slot, mag, offset, shift, work, total):
    lane = iota(1)
    mag = jnp.full((8, 128), mag, jnp.float32)
    for ub in range(TILES):
        u = (lane + 128 * ub).astype(jnp.float32)
        target = (u - CENTRE) / mag + CENTRE + offset
        lower = jnp.floor(target)
        frac = target - lower
        left = lower.astype(jnp.int32)
        right = left + 1
        left_lane, right_lane = left & 127, right & 127
        tiles = FORWARD_TILES[ub]
        for rg in range(ROWS // 8):
            x = [blocks[slot, ROWS * k + 8 * rg : ROWS * k + 8 * rg + 8, :] for k in tiles]
            a, b = take(x[0], left_lane), take(x[0], right_lane)
            for k, tile in zip(tiles[1:], x[1:]):
                a = jnp.where(left >= 128 * k, take(tile, left_lane), a)
                b = jnp.where(right >= 128 * k, take(tile, right_lane), b)
            work[ub, 8 + 8 * rg : 16 + 8 * rg, :] = (1.0 - frac) * a + frac * b
    for ub in range(TILES):
        for rg in range(EXT // 8):
            moved = work[ub, pl.ds(8 + 8 * rg - HALO - shift, 8), :]
            total[ub][rg] = total[ub][rg] + moved


def tap_tables(mag, offset, index_ref, weight_ref, angle):
    lane = iota(1)
    mag = jnp.full((8, 128), mag, jnp.float32)
    for yb in range(TILES):
        y = (lane + 128 * yb).astype(jnp.float32)
        middle = (y - CENTRE - offset) * mag + CENTRE
        for phase in range(2):
            first = jnp.floor((middle - phase) * 0.5).astype(jnp.int32)
            for tap in range(2):
                j = first + tap
                u = (2 * j + phase).astype(jnp.float32)
                target = (u - CENTRE) / mag + CENTRE + offset
                weight = jnp.maximum(0.0, 1.0 - jnp.abs(y - target))
                weight = jnp.where((j >= 0) & (j < 256), weight, 0.0)
                n = 8 * (yb * 4 + phase * 2 + tap)
                index_ref[angle, n : n + 8, :] = jnp.clip(j, 0, 255)
                weight_ref[angle, n : n + 8, :] = weight


def backproject_block(blocks, slot, angle, shift, index_ref, weight_ref, work, total):
    for n in range(0, RES_ROWS, 8):
        work[n : n + 8, :] = blocks[slot, n : n + 8, :]
    for yb in range(TILES):
        n = 32 * yb
        index = [index_ref[angle, n + 8 * t : n + 8 * t + 8, :] for t in range(4)]
        weight = [weight_ref[angle, n + 8 * t : n + 8 * t + 8, :] for t in range(4)]
        lanes = [j & 127 for j in index]
        tiles = BACKWARD_TILES[yb]
        for rg in range(ROWS // 8):
            for phase in range(2):
                start = EXT * phase + HALO + 8 * rg + shift
                x = [work[pl.ds(start + 2 * EXT * k, 8), :] for k in tiles]
                for t in (2 * phase, 2 * phase + 1):
                    value = take(x[0], lanes[t])
                    if len(tiles) == 2:
                        value = jnp.where(index[t] >= 128, take(x[1], lanes[t]), value)
                    total[yb][rg] = total[yb][rg] + weight[t] * value


class Gather:
    def __init__(self, blocks, half_a, half_b, whole, send, recv, place):
        self.blocks, self.send_sem, self.recv_sem = blocks, send, recv
        self.parts = (half_a, half_b, half_a)
        self.half_a, self.half_b, self.whole = half_a, half_b, whole
        self.place = place
        self.sent = []

    def copy(self, source, target, part, n, to):
        rows = pl.ds(*part)
        return pltpu.make_async_remote_copy(
            src_ref=self.blocks.at[source, rows],
            dst_ref=self.blocks.at[target, rows],
            send_sem=self.send_sem.at[n],
            recv_sem=self.recv_sem.at[n],
            device_id={"xband": self.place[to]},
            device_id_type=MESH,
        )

    def send(self, source, target, part, n, to):
        copy = self.copy(source, target, part, n, to)
        copy.start()
        self.sent.append(copy)

    def wait(self, slot, part, n, to):
        self.copy(slot, slot, part, n, to).wait_recv()

    def along(self, way, step, p):
        base = 0 if way == "long" else 4
        source = 0 if step == 0 else base + step
        side = 8 if p == 2 else 0
        n = (0 if way == "long" else 12) + 3 * step + p
        self.send(source + side, base + step + 1 + side, self.parts[p], n, way)

    def start(self):
        self.send(0, 8, self.half_a, 21, "pair")
        self.along("long", 0, 0)
        self.along("short", 0, 0)
        self.along("long", 0, 1)
        self.along("short", 0, 1)
        self.send(0, 8, self.half_b, 22, "pair")
        self.send(0, 16, self.whole, 30, "core")

    def run(self, arrived, group):
        arrived(0)
        self.wait(8, self.half_a, 21, "pair")
        self.along("long", 0, 2)
        self.along("short", 0, 2)
        groups = ((0,), (1, 5), (2, 6), (3, 7), (4,))
        for step in range(1, 7):
            if 2 <= step:
                for r in groups[step - 2]:
                    for side in (0, 8):
                        self.wait(16 + side + r, self.whole, 30 + side + r, "core")
                        arrived(16 + side + r)
            if step <= 4:
                for r in groups[step]:
                    way, last = ("long", 4) if r <= 4 else ("short", 3)
                    first = (0 if r <= 4 else 12) + 3 * (step - 1)
                    for p in range(3):
                        self.wait(r + (8 if p == 2 else 0), self.parts[p], first + p, way)
                        if step < last:
                            self.along(way, step, p)
                        if p == 1:
                            self.send(r, 8 + r, self.half_b, 22 + r, "pair")
                            self.send(r, 16 + r, self.whole, 30 + r, "core")
                            arrived(r)
            if step <= 5:
                for r in groups[step - 1]:
                    self.wait(8 + r, self.half_b, 22 + r, "pair")
                    self.send(8 + r, 24 + r, self.whole, 38 + r, "core")
                    arrived(8 + r)
            if 2 <= step:
                for r in groups[step - 2]:
                    group(r)

    def finish(self):
        for copy in self.sent:
            copy.wait_send()


def load_total(ref, rows):
    return [[ref[t, 8 * g : 8 * g + 8, :] for g in range(rows // 8)] for t in range(TILES)]


def store_total(ref, total):
    for t, groups in enumerate(total):
        for g, value in enumerate(groups):
            ref[t, 8 * g : 8 * g + 8, :] = value


def kernel(
    mag_ref, offset_ref, shift_ref, volume_ref, measured_ref, residual_ref, correction_ref,
    vols, ress, tables, seen, proj, ext, back, sums, below, above, index_ref, weight_ref, image, rows,
    vol_send, vol_recv, res_send, res_recv, slab_send, slab_recv, table_sem,
):
    slab, band = lax.axis_index("zslab"), lax.axis_index("xband")
    half, core = lax.div(band, 16), lax.rem(band, 2)
    z = lax.div(lax.rem(band, 16), 2)
    turn = 1 - 2 * core

    def band_of(half, z, core):
        return half * 16 + lax.rem(z + 2 * RING, RING) * 2 + core

    place = {
        "long": band_of(half, z + turn, core),
        "short": band_of(half, z - turn, core),
        "pair": band_of(1 - half, z, core),
        "core": band_of(half, z, 1 - core),
    }
    barrier = pltpu.get_barrier_semaphore()
    for to in place.values():
        pl.semaphore_signal(barrier, inc=1, device_id={"xband": to}, device_id_type=MESH)
    slabs = [lax.rem(slab + j, SLABS) for j in range(SLABS)]
    for to in slabs[1:]:
        pl.semaphore_signal(barrier, inc=1, device_id={"zslab": to}, device_id_type=MESH)

    lane, row = iota(1), iota(0)

    def spread(angle, values):
        here = lane == angle
        mags, offsets, shifts = values
        return (
            jnp.where(here, mag_ref[angle], mags),
            jnp.where(here, offset_ref[angle].astype(jnp.float32), offsets),
            jnp.where(here, shift_ref[angle].astype(jnp.float32), shifts),
        )

    zeros = jnp.zeros((8, 128), jnp.float32)
    mags, offsets, shifts = lax.fori_loop(0, BANDS, spread, (zeros, zeros, zeros))
    for t in range(TILES):
        vols[0, ROWS * t : ROWS * (t + 1), :] = volume_ref[0, :, 128 * t : 128 * (t + 1)]
        seen[t, 8 : 8 + ROWS, :] = measured_ref[0, :, 128 * t : 128 * (t + 1)]
    vols[0, VOL_ROWS - 8 :, :] = jnp.where(row == 0, mags, jnp.where(row == 1, offsets, shifts))

    pl.semaphore_wait(barrier, 4 + SLABS - 1)

    gather = Gather(vols, VOL_A, VOL_B, VOL_ALL, vol_send, vol_recv, place)
    gather.start()

    def slab_copy(source, target, n, to):
        return pltpu.make_async_remote_copy(
            src_ref=source,
            dst_ref=target,
            send_sem=slab_send.at[n],
            recv_sem=slab_recv.at[n],
            device_id={"zslab": slabs[to]},
            device_id_type=MESH,
        )

    seen_up = slab_copy(seen.at[:, pl.ds(ROWS, 8)], seen.at[:, pl.ds(0, 8)], 0, 1)
    seen_down = slab_copy(seen.at[:, pl.ds(8, 8)], seen.at[:, pl.ds(ROWS + 8, 8)], 1, SLABS - 1)
    seen_up.start()
    seen_down.start()

    for t in range(TILES):
        image[t, 0:8, :] = zeros
        image[t, 8 + ROWS :, :] = zeros
        proj[t] = jnp.zeros((EXT, 128), jnp.float32)
        back[t] = jnp.zeros((ROWS, 128), jnp.float32)

    def fill(angle, carry):
        tap_tables(mag_ref[angle], offset_ref[angle].astype(jnp.float32), index_ref, weight_ref, angle)
        return carry

    lax.fori_loop(0, BANDS, fill, 0)

    def table_copy(slot):
        return pltpu.make_async_copy(
            vols.at[slot, pl.ds(VOL_ROWS - 8, 8)], tables.at[slot], table_sem.at[slot]
        )

    def project_group(r):
        for j in range(4):
            table_copy(r + 8 * j).wait()

        def one(j, carry):
            slot = r + 8 * j
            total = load_total(proj, EXT)
            project_block(
                vols, slot, tables[slot, 0, band], tables[slot, 1, band],
                jnp.clip(tables[slot, 2, band].astype(jnp.int32), -HALO, HALO), image, total,
            )
            store_total(proj, total)
            return carry

        lax.fori_loop(0, 4, one, 0)

    gather.run(lambda slot: table_copy(slot).start(), project_group)

    for t in range(TILES):
        column = jnp.zeros((1, 128), jnp.float32)
        for g in range(EXT // 8):
            value = proj[t, 8 * g : 8 * g + 8, :]
            if g == 0:
                value = jnp.where(row + slab * ROWS >= HALO, value, 0.0)
            if g == EXT // 8 - 1:
                value = jnp.where((row < HALO) | (slab < SLABS - 1), value, 0.0)
            column = column + jnp.sum(value, axis=0, keepdims=True)
        sums[0, t : t + 1, :] = column
        sums[0, TILES + t : TILES + t + 1, :] = jnp.sum(seen[t, 8 : 8 + ROWS, :], axis=0, keepdims=True)
    slab_copies = [seen_up, seen_down]
    for j in range(1, SLABS):
        slab_copies.append(slab_copy(sums.at[0], sums.at[j], 3 + j, j))
    slab_copies.append(slab_copy(proj.at[:, pl.ds(ROWS, 8)], below, 2, 1))
    slab_copies.append(slab_copy(proj.at[:, pl.ds(0, 8)], above, 3, SLABS - 1))
    for copy in slab_copies[2:]:
        copy.start()
    for copy in slab_copies:
        copy.wait_recv()

    all_sums = sums[0]
    for j in range(1, SLABS):
        all_sums = all_sums + sums[j]
    for t in range(TILES):
        gain = all_sums[TILES + t : TILES + t + 1, :] / all_sums[t : t + 1, :]
        gain = jnp.broadcast_to(gain, (8, 128))
        for g in range(EXT // 8):
            value = proj[t, 8 * g : 8 * g + 8, :]
            if g == 0:
                value = value + jnp.where(slab > 0, below[t], 0.0)
            if g == EXT // 8 - 1:
                value = value + jnp.where(slab < SLABS - 1, above[t], 0.0)
            value = (seen[t, 8 * g + HALO : 8 * g + HALO + 8, :] - gain * value) * (1.0 / BANDS)
            if g == 0:
                value = jnp.where(row + slab * ROWS >= HALO, value, 0.0)
            if g == EXT // 8 - 1:
                value = jnp.where((row < HALO) | (slab < SLABS - 1), value, 0.0)
            ext[t, 8 * g : 8 * g + 8, :] = value
    double = 2 * (lane & 63)
    for k in range(2):
        for phase in range(2):
            for g in range(EXT // 8):
                a = take(ext[2 * k, 8 * g : 8 * g + 8, :], double + phase)
                b = take(ext[2 * k + 1, 8 * g : 8 * g + 8, :], double + phase)
                first = 2 * EXT * k + EXT * phase + 8 * g
                ress[0, first : first + 8, :] = jnp.where(lane < 64, a, b)

    spread_out = Gather(ress, RES_A, RES_B, RES_ALL, res_send, res_recv, place)
    spread_out.start()
    for t in range(TILES):
        residual_ref[0, :, 128 * t : 128 * (t + 1)] = ext[t, HALO : HALO + ROWS, :]

    def backproject_group(r):
        away = 0 if r == 0 else (-r if r <= 4 else r - 4)

        def one(j, carry):
            side, plane = lax.rem(j, 2), lax.div(j, 2)
            from_half = half + side - 2 * half * side
            from_core = core + plane - 2 * core * plane
            angle = band_of(from_half, z + away * (1 - 2 * from_core), from_core)
            total = load_total(back, ROWS)
            backproject_block(ress, r + 8 * j, angle, shift_ref[angle], index_ref, weight_ref, rows, total)
            store_total(back, total)
            return carry

        lax.fori_loop(0, 4, one, 0)

    spread_out.run(lambda slot: None, backproject_group)
    for t in range(TILES):
        correction_ref[0, :, 128 * t : 128 * (t + 1)] = back[t] * (1.0 / math.sqrt(BANDS))
    gather.finish()
    spread_out.finish()
    for copy in slab_copies:
        copy.wait_send()


def shards(volume, measured, magnification, shift_y, shift_z):
    smem, vmem = pl.BlockSpec(memory_space=pltpu.SMEM), pl.BlockSpec(memory_space=pltpu.VMEM)
    block = jax.ShapeDtypeStruct(volume.shape, jnp.float32)
    f32 = jnp.float32
    return pl.pallas_call(
        kernel,
        out_shape=(block, block),
        in_specs=[smem, smem, smem, vmem, vmem],
        out_specs=(vmem, vmem),
        scratch_shapes=[
            pltpu.VMEM((BANDS, VOL_ROWS, 128), f32),
            pltpu.VMEM((BANDS, RES_ROWS, 128), f32),
            pltpu.SMEM((BANDS, 8, 128), f32),
            pltpu.VMEM((TILES, ROWS + 16, 128), f32),
            pltpu.VMEM((TILES, EXT, 128), f32),
            pltpu.VMEM((TILES, EXT, 128), f32),
            pltpu.VMEM((TILES, ROWS, 128), f32),
            pltpu.VMEM((SLABS, 8, 128), f32),
            pltpu.VMEM((TILES, 8, 128), f32),
            pltpu.VMEM((TILES, 8, 128), f32),
            pltpu.VMEM((BANDS, 128, 128), jnp.int32),
            pltpu.VMEM((BANDS, 128, 128), f32),
            pltpu.VMEM((TILES, ROWS + 16, 128), f32),
            pltpu.VMEM((RES_ROWS, 128), f32),
            pltpu.SemaphoreType.DMA((COPIES,)),
            pltpu.SemaphoreType.DMA((COPIES,)),
            pltpu.SemaphoreType.DMA((COPIES,)),
            pltpu.SemaphoreType.DMA((COPIES,)),
            pltpu.SemaphoreType.DMA((SLABS + 3,)),
            pltpu.SemaphoreType.DMA((SLABS + 3,)),
            pltpu.SemaphoreType.DMA((BANDS,)),
        ],
        compiler_params=pltpu.CompilerParams(
            collective_id=0, has_side_effects=True, vmem_limit_bytes=40 * 1024 * 1024
        ),
        name="sirt",
    )(
        magnification.reshape(BANDS),
        shift_y.reshape(BANDS),
        shift_z.reshape(BANDS),
        volume,
        measured,
    )


def solution(mesh):
    return jax.shard_map(
        shards,
        mesh=mesh,
        in_specs=(
            P("xband", "zslab", None),
            P("xband", "zslab", None),
            P(None, "xband"),
            P(None, "xband"),
            P(None, "xband"),
        ),
        out_specs=(P("xband", "zslab", None), P("xband", "zslab", None)),
        check_vma=False,
    )
```

```python
import math

import jax
import jax.numpy as jnp
from jax import lax
from jax.experimental import pallas as pl
from jax.experimental.pallas import tpu as pltpu
from jax.sharding import PartitionSpec as P

HALO = 4
TILES = 4
ROWS = 32
EXT = ROWS + 2 * HALO
SLABS = 8
RING = 8
BANDS = 32
CENTRE = 255.5
VOL_ROWS = TILES * ROWS + 8
RES_ROWS = TILES * EXT
VOL_PARTS = ((0, 64), (64, 72), (0, 136))
RES_PARTS = ((0, 80), (80, 80), (0, 160))
COPIES = 20
COLUMN = 16
FORWARD_TILES = ((0, 1), (0, 1, 2), (1, 2, 3), (2, 3))
BACKWARD_TILES = ((0,), (0, 1), (0, 1), (1,))
MESH = pl.DeviceIdType.MESH


def take(x, index):
    return jnp.take_along_axis(x, index, axis=1, mode="promise_in_bounds")


def iota(axis):
    return lax.broadcasted_iota(jnp.int32, (8, 128), axis)


def project_block(blocks, slot, mag, offset, shift, work, total):
    lane = iota(1)
    mag = jnp.full((8, 128), mag, jnp.float32)
    for ub in range(TILES):
        u = (lane + 128 * ub).astype(jnp.float32)
        target = (u - CENTRE) / mag + CENTRE + offset
        lower = jnp.floor(target)
        frac = target - lower
        left = lower.astype(jnp.int32)
        right = left + 1
        left_lane, right_lane = left & 127, right & 127
        tiles = FORWARD_TILES[ub]
        for rg in range(ROWS // 8):
            x = [blocks[slot, ROWS * k + 8 * rg : ROWS * k + 8 * rg + 8, :] for k in tiles]
            a, b = take(x[0], left_lane), take(x[0], right_lane)
            for k, tile in zip(tiles[1:], x[1:]):
                a = jnp.where(left >= 128 * k, take(tile, left_lane), a)
                b = jnp.where(right >= 128 * k, take(tile, right_lane), b)
            work[ub, 8 + 8 * rg : 16 + 8 * rg, :] = (1.0 - frac) * a + frac * b
    for ub in range(TILES):
        for rg in range(EXT // 8):
            moved = work[ub, pl.ds(8 + 8 * rg - HALO - shift, 8), :]
            total[ub][rg] = total[ub][rg] + moved


def tap_tables(mag, offset, index_ref, weight_ref, angle):
    lane = iota(1)
    mag = jnp.full((8, 128), mag, jnp.float32)
    for yb in range(TILES):
        y = (lane + 128 * yb).astype(jnp.float32)
        middle = (y - CENTRE - offset) * mag + CENTRE
        for phase in range(2):
            first = jnp.floor((middle - phase) * 0.5).astype(jnp.int32)
            for tap in range(2):
                j = first + tap
                u = (2 * j + phase).astype(jnp.float32)
                target = (u - CENTRE) / mag + CENTRE + offset
                weight = jnp.maximum(0.0, 1.0 - jnp.abs(y - target))
                weight = jnp.where((j >= 0) & (j < 256), weight, 0.0)
                n = 8 * (yb * 4 + phase * 2 + tap)
                index_ref[angle, n : n + 8, :] = jnp.clip(j, 0, 255)
                weight_ref[angle, n : n + 8, :] = weight


def backproject_block(blocks, slot, angle, shift, index_ref, weight_ref, work, total):
    for n in range(0, RES_ROWS, 8):
        work[n : n + 8, :] = blocks[slot, n : n + 8, :]
    for yb in range(TILES):
        n = 32 * yb
        index = [index_ref[angle, n + 8 * t : n + 8 * t + 8, :] for t in range(4)]
        weight = [weight_ref[angle, n + 8 * t : n + 8 * t + 8, :] for t in range(4)]
        lanes = [j & 127 for j in index]
        tiles = BACKWARD_TILES[yb]
        for rg in range(ROWS // 8):
            for phase in range(2):
                start = EXT * phase + HALO + 8 * rg + shift
                x = [work[pl.ds(start + 2 * EXT * k, 8), :] for k in tiles]
                for t in (2 * phase, 2 * phase + 1):
                    value = take(x[0], lanes[t])
                    if len(tiles) == 2:
                        value = jnp.where(index[t] >= 128, take(x[1], lanes[t]), value)
                    total[yb][rg] = total[yb][rg] + weight[t] * value


class Gather:
    def __init__(self, blocks, parts, send, recv, place):
        self.blocks, self.parts, self.send_sem, self.recv_sem = blocks, parts, send, recv
        self.place = place
        self.sent = []

    def copy(self, source, target, part, n, to):
        rows = pl.ds(*self.parts[part])
        return pltpu.make_async_remote_copy(
            src_ref=self.blocks.at[source, rows],
            dst_ref=self.blocks.at[target, rows],
            send_sem=self.send_sem.at[n],
            recv_sem=self.recv_sem.at[n],
            device_id={"xband": self.place[to]},
            device_id_type=MESH,
        )

    def send(self, source, target, part, n, to):
        copy = self.copy(source, target, part, n, to)
        copy.start()
        self.sent.append(copy)

    def wait(self, slot, part, n):
        self.copy(slot, slot, part, n, "core").wait_recv()

    def start(self):
        for part in range(2):
            self.send(0, 2, part, 2 + part, "long2")
            self.send(0, 6, part, 4 + part, "short2")
        self.send(0, 1, 2, 0, "long1")
        self.send(0, 5, 2, 1, "short1")
        self.send(0, 8, 2, 12, "core")

    def core(self, r):
        self.send(r, 8 + r, 2, 12 + r, "core")

    def run(self, arrived, compute, meanwhile):
        arrived(0)
        compute(0)
        self.wait(8, 2, 12)
        arrived(8)
        compute(8)
        for part in range(2):
            self.wait(2, part, 2 + part)
            self.send(2, 4, part, 8 + part, "long2")
            self.send(2, 3, part, 6 + part, "long1")
            self.wait(6, part, 4 + part)
            self.send(6, 7, part, 10 + part, "short1")
        self.core(2)
        self.core(6)
        for n, r in enumerate((1, 5)):
            self.wait(r, 2, n)
            self.core(r)
        for r in (1, 5, 2, 6):
            arrived(r)
        meanwhile()
        for r in (1, 5, 2, 6):
            compute(r)
        for r in (2, 6, 1, 5):
            self.wait(8 + r, 2, 12 + r)
            arrived(8 + r)
        for r in (9, 13):
            compute(r)
        for r, n in ((3, 6), (7, 10), (4, 8)):
            self.wait(r, 0, n)
            self.wait(r, 1, n + 1)
            self.core(r)
            arrived(r)
        for r in (10, 14, 3, 7, 4):
            compute(r)
        for r in (3, 7, 4):
            self.wait(8 + r, 2, 12 + r)
            arrived(8 + r)
        for r in (11, 15, 12):
            compute(r)

    def finish(self):
        for copy in self.sent:
            copy.wait_send()


def load_total(ref, q, rows):
    return [[ref[q, t, 8 * g : 8 * g + 8, :] for g in range(rows // 8)] for t in range(TILES)]


def store_total(ref, q, total):
    for t, groups in enumerate(total):
        for g, value in enumerate(groups):
            ref[q, t, 8 * g : 8 * g + 8, :] = value


def kernel(
    mag_ref, offset_ref, shift_ref, volume_ref, measured_ref, residual_ref, correction_ref,
    vols, ress, tables, pair_vmem, pair_ref, seen, proj, other, ext, back, other_back, own_sums, sums, below, above,
    index_ref, weight_ref, image, rows,
    vol_send, vol_recv, res_send, res_recv, slab_send, slab_recv, pair_send, pair_recv, table_sem,
):
    slab, band = lax.axis_index("zslab"), lax.axis_index("xband")
    half, core = lax.div(band, 16), lax.rem(band, 2)
    z = lax.div(lax.rem(band, 16), 2)
    turn = 1 - 2 * core
    pair = (1 - half) * COLUMN + lax.rem(band, COLUMN)

    def ring(away):
        return half * COLUMN + lax.rem(z + away + 2 * RING, RING) * 2 + core

    place = {
        "long1": ring(turn),
        "long2": ring(2 * turn),
        "short1": ring(-turn),
        "short2": ring(-2 * turn),
        "core": band + turn,
        "pair": pair,
    }
    barrier = pltpu.get_barrier_semaphore()
    for to in place.values():
        pl.semaphore_signal(barrier, inc=1, device_id={"xband": to}, device_id_type=MESH)
    slabs = [lax.rem(slab + j, SLABS) for j in range(SLABS)]
    for to in slabs[1:]:
        for of in (band, pair):
            pl.semaphore_signal(barrier, inc=1, device_id={"zslab": to, "xband": of}, device_id_type=MESH)

    lane, row = iota(1), iota(0)

    def spread(angle, values):
        here = lane == angle
        mags, offsets, shifts = values
        return (
            jnp.where(here, mag_ref[angle], mags),
            jnp.where(here, offset_ref[angle].astype(jnp.float32), offsets),
            jnp.where(here, shift_ref[angle].astype(jnp.float32), shifts),
        )

    zeros = jnp.zeros((8, 128), jnp.float32)
    mags, offsets, shifts = lax.fori_loop(0, BANDS, spread, (zeros, zeros, zeros))
    for t in range(TILES):
        vols[0, ROWS * t : ROWS * (t + 1), :] = volume_ref[0, :, 128 * t : 128 * (t + 1)]
        seen[t, 8 : 8 + ROWS, :] = measured_ref[0, :, 128 * t : 128 * (t + 1)]
    vols[0, VOL_ROWS - 8 :, :] = jnp.where(row == 0, mags, jnp.where(row == 1, offsets, shifts))

    pl.semaphore_wait(barrier, 6 + 2 * (SLABS - 1))

    gather = Gather(vols, VOL_PARTS, vol_send, vol_recv, place)
    gather.start()

    def pair_copy(source, target, n):
        return pltpu.make_async_remote_copy(
            src_ref=source,
            dst_ref=target,
            send_sem=pair_send.at[n],
            recv_sem=pair_recv.at[n],
            device_id={"xband": pair},
            device_id_type=MESH,
        )

    def slab_copy(source, target, n, to, of=band):
        return pltpu.make_async_remote_copy(
            src_ref=source,
            dst_ref=target,
            send_sem=slab_send.at[n],
            recv_sem=slab_recv.at[n],
            device_id={"zslab": slabs[to], "xband": of},
            device_id_type=MESH,
        )

    pair_values = pair_copy(vols.at[0, pl.ds(VOL_ROWS - 8, 8)], pair_vmem, 0)
    pair_values.start()
    seen_up = slab_copy(seen.at[:, pl.ds(ROWS, 8)], seen.at[:, pl.ds(0, 8)], 0, 1)
    seen_down = slab_copy(seen.at[:, pl.ds(8, 8)], seen.at[:, pl.ds(ROWS + 8, 8)], 1, SLABS - 1)
    seen_up.start()
    seen_down.start()

    for t in range(TILES):
        image[t, 0:8, :] = zeros
        image[t, 8 + ROWS :, :] = zeros
        for q in range(2):
            proj[q, t] = jnp.zeros((EXT, 128), jnp.float32)
            back[q, t] = jnp.zeros((ROWS, 128), jnp.float32)

    def fill_own(n, carry):
        angle = half * COLUMN + n
        tap_tables(mag_ref[angle], offset_ref[angle].astype(jnp.float32), index_ref, weight_ref, 2 * n)
        return carry

    lax.fori_loop(0, COLUMN, fill_own, 0)

    def fill_pair():
        pair_values.wait_recv()
        local = pltpu.make_async_copy(pair_vmem, pair_ref, table_sem.at[COLUMN])
        local.start()
        local.wait()

        def one(n, carry):
            angle = half * COLUMN + n
            tap_tables(pair_ref[0, angle], pair_ref[1, angle], index_ref, weight_ref, 2 * n + 1)
            return carry

        lax.fori_loop(0, COLUMN, one, 0)

    def table_copy(slot):
        return pltpu.make_async_copy(
            vols.at[slot, pl.ds(VOL_ROWS - 8, 8)], tables.at[slot], table_sem.at[slot]
        )

    def project(slot):
        table_copy(slot).wait()

        def one(q, carry):
            angle = band + q * (pair - band)
            shift = jnp.clip(tables[slot, 2, angle].astype(jnp.int32), -HALO, HALO)
            total = load_total(proj, q, EXT)
            project_block(vols, slot, tables[slot, 0, angle], tables[slot, 1, angle], shift, image, total)
            store_total(proj, q, total)
            return carry

        lax.fori_loop(0, 2, one, 0)

    gather.run(lambda slot: table_copy(slot).start(), project, fill_pair)

    exchange = [
        pair_copy(proj.at[1], other, 1),
        slab_copy(proj.at[0, :, pl.ds(ROWS, 8)], below.at[0], 2, 1),
        slab_copy(proj.at[0, :, pl.ds(0, 8)], above.at[0], 3, SLABS - 1),
        slab_copy(proj.at[1, :, pl.ds(ROWS, 8)], below.at[1], 4, 1, pair),
        slab_copy(proj.at[1, :, pl.ds(0, 8)], above.at[1], 5, SLABS - 1, pair),
    ]
    for copy in exchange:
        copy.start()
    for q in range(2):
        for t in range(TILES):
            column = jnp.zeros((1, 128), jnp.float32)
            for g in range(EXT // 8):
                value = proj[q, t, 8 * g : 8 * g + 8, :]
                if g == 0:
                    value = jnp.where(row + slab * ROWS >= HALO, value, 0.0)
                if g == EXT // 8 - 1:
                    value = jnp.where((row < HALO) | (slab < SLABS - 1), value, 0.0)
                column = column + jnp.sum(value, axis=0, keepdims=True)
            own_sums[q, t : t + 1, :] = column
            if q == 0:
                column = jnp.sum(seen[t, 8 : 8 + ROWS, :], axis=0, keepdims=True)
            else:
                column = jnp.zeros((1, 128), jnp.float32)
            own_sums[q, TILES + t : TILES + t + 1, :] = column
        for j in range(1 - q, SLABS):
            n = 5 + j + 7 * q + q
            if j == 0:
                copy = pair_copy(own_sums.at[1], sums.at[SLABS], 2)
            else:
                copy = slab_copy(own_sums.at[q], sums.at[SLABS * q + j], n, j, pair if q else band)
            copy.start()
            exchange.append(copy)
    for copy in [seen_up, seen_down] + exchange:
        copy.wait_recv()

    all_sums = own_sums[0]
    for j in range(1, 2 * SLABS):
        all_sums = all_sums + sums[j]
    for t in range(TILES):
        gain = all_sums[TILES + t : TILES + t + 1, :] / all_sums[t : t + 1, :]
        gain = jnp.broadcast_to(gain, (8, 128))
        for g in range(EXT // 8):
            value = proj[0, t, 8 * g : 8 * g + 8, :] + other[t, 8 * g : 8 * g + 8, :]
            if g == 0:
                value = value + jnp.where(slab > 0, below[0, t] + below[1, t], 0.0)
            if g == EXT // 8 - 1:
                value = value + jnp.where(slab < SLABS - 1, above[0, t] + above[1, t], 0.0)
            value = (seen[t, 8 * g + HALO : 8 * g + HALO + 8, :] - gain * value) * (1.0 / BANDS)
            if g == 0:
                value = jnp.where(row + slab * ROWS >= HALO, value, 0.0)
            if g == EXT // 8 - 1:
                value = jnp.where((row < HALO) | (slab < SLABS - 1), value, 0.0)
            ext[t, 8 * g : 8 * g + 8, :] = value
    double = 2 * (lane & 63)
    for k in range(2):
        for phase in range(2):
            for g in range(EXT // 8):
                a = take(ext[2 * k, 8 * g : 8 * g + 8, :], double + phase)
                b = take(ext[2 * k + 1, 8 * g : 8 * g + 8, :], double + phase)
                first = 2 * EXT * k + EXT * phase + 8 * g
                ress[0, first : first + 8, :] = jnp.where(lane < 64, a, b)

    spread_out = Gather(ress, RES_PARTS, res_send, res_recv, place)
    spread_out.start()
    for t in range(TILES):
        residual_ref[0, :, 128 * t : 128 * (t + 1)] = ext[t, HALO : HALO + ROWS, :]

    def backproject(slot):
        r, from_core = slot % 8, core if slot < 8 else 1 - core
        away = -r if r <= 4 else r - 4
        local = lax.rem(z + away * (1 - 2 * from_core) + 2 * RING, RING) * 2 + from_core
        angle = half * COLUMN + local

        def one(q, carry):
            shift = jnp.where(q == 0, shift_ref[angle], pair_ref[2, angle].astype(jnp.int32))
            shift = jnp.clip(shift, -HALO, HALO)
            total = load_total(back, q, ROWS)
            backproject_block(ress, slot, 2 * local + q, shift, index_ref, weight_ref, rows, total)
            store_total(back, q, total)
            return carry

        lax.fori_loop(0, 2, one, 0)

    spread_out.run(lambda slot: None, backproject, lambda: None)
    last = pair_copy(back.at[1], other_back, 3)
    last.start()
    last.wait_recv()
    for t in range(TILES):
        value = (back[0, t] + other_back[t]) * (1.0 / math.sqrt(BANDS))
        correction_ref[0, :, 128 * t : 128 * (t + 1)] = value
    gather.finish()
    spread_out.finish()
    for copy in [pair_values, seen_up, seen_down, last] + exchange:
        copy.wait_send()


def shards(volume, measured, magnification, shift_y, shift_z):
    smem, vmem = pl.BlockSpec(memory_space=pltpu.SMEM), pl.BlockSpec(memory_space=pltpu.VMEM)
    block = jax.ShapeDtypeStruct(volume.shape, jnp.float32)
    f32 = jnp.float32
    return pl.pallas_call(
        kernel,
        out_shape=(block, block),
        in_specs=[smem, smem, smem, vmem, vmem],
        out_specs=(vmem, vmem),
        scratch_shapes=[
            pltpu.VMEM((COLUMN, VOL_ROWS, 128), f32),
            pltpu.VMEM((COLUMN, RES_ROWS, 128), f32),
            pltpu.SMEM((COLUMN, 8, 128), f32),
            pltpu.VMEM((8, 128), f32),
            pltpu.SMEM((8, 128), f32),
            pltpu.VMEM((TILES, ROWS + 16, 128), f32),
            pltpu.VMEM((2, TILES, EXT, 128), f32),
            pltpu.VMEM((TILES, EXT, 128), f32),
            pltpu.VMEM((TILES, EXT, 128), f32),
            pltpu.VMEM((2, TILES, ROWS, 128), f32),
            pltpu.VMEM((TILES, ROWS, 128), f32),
            pltpu.VMEM((2, 8, 128), f32),
            pltpu.VMEM((2 * SLABS, 8, 128), f32),
            pltpu.VMEM((2, TILES, 8, 128), f32),
            pltpu.VMEM((2, TILES, 8, 128), f32),
            pltpu.VMEM((BANDS, 128, 128), jnp.int32),
            pltpu.VMEM((BANDS, 128, 128), f32),
            pltpu.VMEM((TILES, ROWS + 16, 128), f32),
            pltpu.VMEM((RES_ROWS, 128), f32),
            pltpu.SemaphoreType.DMA((COPIES,)),
            pltpu.SemaphoreType.DMA((COPIES,)),
            pltpu.SemaphoreType.DMA((COPIES,)),
            pltpu.SemaphoreType.DMA((COPIES,)),
            pltpu.SemaphoreType.DMA((2 * SLABS + 5,)),
            pltpu.SemaphoreType.DMA((2 * SLABS + 5,)),
            pltpu.SemaphoreType.DMA((4,)),
            pltpu.SemaphoreType.DMA((4,)),
            pltpu.SemaphoreType.DMA((COLUMN + 1,)),
        ],
        compiler_params=pltpu.CompilerParams(
            collective_id=0, has_side_effects=True, vmem_limit_bytes=40 * 1024 * 1024
        ),
        name="sirt",
    )(
        magnification.reshape(BANDS),
        shift_y.reshape(BANDS),
        shift_z.reshape(BANDS),
        volume,
        measured,
    )


def solution(mesh):
    return jax.shard_map(
        shards,
        mesh=mesh,
        in_specs=(
            P("xband", "zslab", None),
            P("xband", "zslab", None),
            P(None, "xband"),
            P(None, "xband"),
            P(None, "xband"),
        ),
        out_specs=(P("xband", "zslab", None), P("xband", "zslab", None)),
        check_vma=False,
    )
```

```python
import functools
import math

import jax
import jax.numpy as jnp
from jax import lax
from jax.experimental import pallas as pl
from jax.experimental.pallas import tpu as pltpu
from jax.sharding import PartitionSpec as P

HALO = 4
TILES = 4
ROWS = 32
EXT = ROWS + 2 * HALO
SLABS = 8
RING = 8
BANDS = 32
CENTRE = 255.5
RES_ROWS = TILES * EXT
VOL_PARTS = ((0, 16), (16, 16), (0, 32))
RES_PARTS = ((0, 80), (80, 80), (0, 160))
COPIES = 20
COLUMN = 16
FORWARD_TILES = ((0, 1), (0, 1, 2), (1, 2, 3), (2, 3))
BACKWARD_TILES = ((0,), (0, 1), (0, 1), (1,))
MESH = pl.DeviceIdType.MESH


def take(x, index):
    return jnp.take_along_axis(x, index, axis=1, mode="promise_in_bounds")


def iota(axis):
    return lax.broadcasted_iota(jnp.int32, (8, 128), axis)


def take_tiles(tiles, index):
    lanes = index & 127
    values = None
    for k, groups in tiles.items():
        part = [take(x, lanes) for x in groups]
        if values is None:
            values = part
        else:
            here = index >= 128 * k
            values = [jnp.where(here, p, v) for p, v in zip(part, values)]
    return values


def project_block(blocks, slot, mag, offset, shift, work, total):
    lane = iota(1)
    mag = jnp.full((8, 128), mag, jnp.float32)
    for ub in range(TILES):
        u = (lane + 128 * ub).astype(jnp.float32)
        target = (u - CENTRE) / mag + CENTRE + offset
        lower = jnp.floor(target)
        frac = target - lower
        left = lower.astype(jnp.int32)
        tiles = {
            k: [blocks[slot, 8 * g : 8 * g + 8, 128 * k : 128 * k + 128] for g in range(ROWS // 8)]
            for k in FORWARD_TILES[ub]
        }
        a = take_tiles(tiles, left)
        b = take_tiles(tiles, left + 1)
        for g in range(ROWS // 8):
            work[ub, 8 + 8 * g : 16 + 8 * g, :] = (1.0 - frac) * a[g] + frac * b[g]
    for ub in range(TILES):
        for rg in range(EXT // 8):
            moved = work[ub, pl.ds(8 + 8 * rg - HALO - shift, 8), :]
            total[ub][rg] = total[ub][rg] + moved


def tap_tables(mag, offset, index_ref, weight_ref, angle):
    lane = iota(1)
    mag = jnp.full((8, 128), mag, jnp.float32)
    for yb in range(TILES):
        y = (lane + 128 * yb).astype(jnp.float32)
        middle = (y - CENTRE - offset) * mag + CENTRE
        for phase in range(2):
            first = jnp.floor((middle - phase) * 0.5).astype(jnp.int32)
            for tap in range(2):
                j = first + tap
                u = (2 * j + phase).astype(jnp.float32)
                target = (u - CENTRE) / mag + CENTRE + offset
                weight = jnp.maximum(0.0, 1.0 - jnp.abs(y - target))
                weight = jnp.where((j >= 0) & (j < 256), weight, 0.0)
                n = 8 * (yb * 4 + phase * 2 + tap)
                index_ref[angle, n : n + 8, :] = jnp.clip(j, 0, 255)
                weight_ref[angle, n : n + 8, :] = weight


def backproject_block(angle, shift, index_ref, weight_ref, work, total):
    for yb in range(TILES):
        for phase in range(2):
            start = EXT * phase + HALO + shift
            tiles = {
                k: [work[pl.ds(start + 2 * EXT * k + 8 * g, 8), :] for g in range(ROWS // 8)]
                for k in BACKWARD_TILES[yb]
            }
            for tap in range(2):
                n = 8 * (4 * yb + 2 * phase + tap)
                values = take_tiles(tiles, index_ref[angle, n : n + 8, :])
                weight = weight_ref[angle, n : n + 8, :]
                total[yb] = [t + weight * v for t, v in zip(total[yb], values)]


OWN = (0, 2, 3, 4, 5, 10, 11, 12)
OTHER = (1, 6, 7, 8, 9, 13, 14, 15)
AWAY = (0, 1, -1, 2, -2, 3, -3, 4)


class Gather:
    def __init__(self, blocks, parts, send, recv, place, own=None):
        self.blocks, self.parts, self.send_sem, self.recv_sem = blocks, parts, send, recv
        self.place = place
        self.own = blocks.at[0] if own is None else own
        self.sent = []

    def copy(self, source, target, part, n, to):
        rows = pl.ds(*self.parts[part])
        return pltpu.make_async_remote_copy(
            src_ref=source.at[rows],
            dst_ref=self.blocks.at[target, rows],
            send_sem=self.send_sem.at[n],
            recv_sem=self.recv_sem.at[n],
            device_id={"xband": self.place[to]},
            device_id_type=MESH,
        )

    def send(self, source, target, part, n, to):
        self.copy(self.blocks.at[source] if source else self.own, target, part, n, to).start()
        self.sent.append((source, target, part, n, to))

    def wait(self, slot, part, n):
        self.copy(self.blocks.at[slot], slot, part, n, "core").wait_recv()

    def start(self):
        for part in range(2):
            self.send(0, OWN[3], part, 2 + part, "long2")
            self.send(0, OWN[4], part, 4 + part, "short2")
        self.send(0, OWN[1], 2, 0, "long1")
        self.send(0, OWN[2], 2, 1, "short1")
        self.core(0)

    def core(self, p):
        self.send(OWN[p], OTHER[p], 2, 12 + p, "core")

    def from_core(self, p):
        self.wait(OTHER[p], 2, 12 + p)

    def run(self, compute, between):
        def first():
            for part in range(2):
                self.wait(OWN[3], part, 2 + part)
                self.send(OWN[3], OWN[7], part, 8 + part, "long2")
                self.send(OWN[3], OWN[5], part, 6 + part, "long1")
                self.wait(OWN[4], part, 4 + part)
                self.send(OWN[4], OWN[6], part, 10 + part, "short1")
            self.core(3)
            self.core(4)
            for n, p in enumerate((1, 2)):
                self.wait(OWN[p], 2, n)
                self.core(p)
            between()
            self.from_core(0)

        def last():
            for p, n in ((5, 6), (6, 10), (7, 8)):
                self.wait(OWN[p], 0, n)
                self.wait(OWN[p], 1, n + 1)
                self.core(p)

        actions = {1: first, OWN[5]: last}
        for p in range(1, RING):
            actions[OTHER[p]] = functools.partial(self.from_core, p)

        def one(slot, carry):
            for n, action in actions.items():
                pl.when(slot == n)(action)
            compute(slot)
            return carry

        lax.fori_loop(0, COLUMN, one, 0)

    def finish(self):
        for source, *rest in self.sent:
            self.copy(self.blocks.at[source] if source else self.own, *rest).wait_send()


def load_total(ref, q, rows):
    return [[ref[q, t, 8 * g : 8 * g + 8, :] for g in range(rows // 8)] for t in range(TILES)]


def store_total(ref, q, total):
    for t, groups in enumerate(total):
        for g, value in enumerate(groups):
            ref[q, t, 8 * g : 8 * g + 8, :] = value


def kernel(
    mag_hbm, offset_hbm, shift_hbm, volume_ref, measured_ref, residual_ref, correction_ref,
    mag_ref, offset_ref, shift_ref, order,
    vols, ress, tables_vmem, tables, pair_vmem, pair_ref, seen, proj, other, ext, back, other_back, own_sums, sums,
    below, above, index_ref, weight_ref, image_0, image_1, rows,
    vol_send, vol_recv, res_send, res_recv, slab_send, slab_recv, pair_send, pair_recv,
    values_send, values_recv, local_sem,
):
    slab, band = lax.axis_index("zslab"), lax.axis_index("xband")
    half, core = lax.div(band, 16), lax.rem(band, 2)
    z = lax.div(lax.rem(band, 16), 2)
    turn = 1 - 2 * core
    pair = (1 - half) * COLUMN + lax.rem(band, COLUMN)

    def ring(away, core=core):
        return half * COLUMN + lax.rem(z + away + 2 * RING, RING) * 2 + core

    scalars = [
        pltpu.make_async_copy(source, target, local_sem.at[n])
        for n, (source, target) in enumerate(
            ((mag_hbm, mag_ref), (offset_hbm, offset_ref), (shift_hbm, shift_ref))
        )
    ]
    own_block = pltpu.make_async_copy(volume_ref.at[0], vols.at[0], local_sem.at[3])
    own_seen = [
        pltpu.make_async_copy(
            measured_ref.at[0, :, pl.ds(128 * t, 128)], seen.at[t, pl.ds(8, ROWS)], local_sem.at[4 + t]
        )
        for t in range(TILES)
    ]
    for copy in [*scalars, own_block, *own_seen]:
        copy.start()

    place = {
        "long1": ring(turn),
        "long2": ring(2 * turn),
        "short1": ring(-turn),
        "short2": ring(-2 * turn),
        "core": band + turn,
        "pair": pair,
    }
    column = {}
    for p, away in enumerate(AWAY):
        column[OWN[p]], column[OTHER[p]] = ring(turn * away), ring(turn * away, 1 - core)
    del column[0]
    for p, away in enumerate(AWAY):
        order[OWN[p]] = lax.rem(z - turn * away + 2 * RING, RING) * 2 + core
        order[OTHER[p]] = lax.rem(z + turn * away + 2 * RING, RING) * 2 + 1 - core
    barrier = pltpu.get_barrier_semaphore()
    for to in [*column.values(), pair]:
        pl.semaphore_signal(barrier, inc=1, device_id={"xband": to}, device_id_type=MESH)
    slabs = [lax.rem(slab + j, SLABS) for j in range(SLABS)]
    for to in slabs[1:]:
        for of in (band, pair):
            pl.semaphore_signal(barrier, inc=1, device_id={"zslab": to, "xband": of}, device_id_type=MESH)

    lane, row = iota(1), iota(0)
    for copy in scalars:
        copy.wait()

    def spread(angle, values):
        here = lane == angle
        mags, offsets, shifts = values
        return (
            jnp.where(here, mag_ref[angle], mags),
            jnp.where(here, offset_ref[angle].astype(jnp.float32), offsets),
            jnp.where(here, shift_ref[angle].astype(jnp.float32), shifts),
        )

    zeros = jnp.zeros((8, 128), jnp.float32)
    mags, offsets, shifts = lax.fori_loop(0, BANDS, spread, (zeros, zeros, zeros))
    tables_vmem[0] = jnp.where(row == 0, mags, jnp.where(row == 1, offsets, shifts))

    pl.semaphore_wait(barrier, COLUMN + 2 * (SLABS - 1))

    gather = Gather(vols, VOL_PARTS, vol_send, vol_recv, place, volume_ref.at[0])
    gather.start()

    def pair_copy(source, target, n):
        return pltpu.make_async_remote_copy(
            src_ref=source,
            dst_ref=target,
            send_sem=pair_send.at[n],
            recv_sem=pair_recv.at[n],
            device_id={"xband": pair},
            device_id_type=MESH,
        )

    def slab_copy(source, target, n, to, of=band):
        return pltpu.make_async_remote_copy(
            src_ref=source,
            dst_ref=target,
            send_sem=slab_send.at[n],
            recv_sem=slab_recv.at[n],
            device_id={"zslab": slabs[to], "xband": of},
            device_id_type=MESH,
        )

    pair_values = pair_copy(tables_vmem.at[0], pair_vmem, 0)
    pair_values.start()
    values = [
        pltpu.make_async_remote_copy(
            src_ref=tables_vmem.at[0],
            dst_ref=tables_vmem.at[r],
            send_sem=values_send.at[r],
            recv_sem=values_recv.at[r],
            device_id={"xband": to},
            device_id_type=MESH,
        )
        for r, to in column.items()
    ]
    for copy in values:
        copy.start()
    own_table = pltpu.make_async_copy(tables_vmem.at[0], tables.at[0], local_sem.at[0])
    own_table.start()
    for copy in own_seen:
        copy.wait()
    seen_up = slab_copy(seen.at[:, pl.ds(ROWS, 8)], seen.at[:, pl.ds(0, 8)], 0, 1)
    seen_down = slab_copy(seen.at[:, pl.ds(8, 8)], seen.at[:, pl.ds(ROWS + 8, 8)], 1, SLABS - 1)
    seen_up.start()
    seen_down.start()

    for t in range(TILES):
        for image in (image_0, image_1):
            image[t, 0:8, :] = zeros
            image[t, 8 + ROWS :, :] = zeros
        for q in range(2):
            proj[q, t] = jnp.zeros((EXT, 128), jnp.float32)
            back[q, t] = jnp.zeros((ROWS, 128), jnp.float32)

    def fill_own(n, carry):
        angle = half * COLUMN + order[n]
        tap_tables(mag_ref[angle], offset_ref[angle].astype(jnp.float32), index_ref, weight_ref, 2 * n)
        return carry

    lax.fori_loop(0, COLUMN, fill_own, 0)

    def between():
        for copy in [pair_values, *values]:
            copy.wait_recv()
        local = [
            pltpu.make_async_copy(pair_vmem, pair_ref, local_sem.at[1]),
            pltpu.make_async_copy(
                tables_vmem.at[pl.ds(1, COLUMN - 1)], tables.at[pl.ds(1, COLUMN - 1)], local_sem.at[2]
            ),
        ]
        for copy in local:
            copy.start()
        for copy in local:
            copy.wait()

    def fill_pair():
        def one(n, carry):
            angle = half * COLUMN + order[n]
            tap_tables(pair_ref[0, angle], pair_ref[1, angle], index_ref, weight_ref, 2 * n + 1)
            return carry

        lax.fori_loop(0, COLUMN, one, 0)

    def project(slot):
        for q in range(2):
            angle = pair if q else band
            mag, offset, shift = (tables[slot, n, angle] for n in range(3))
            shift = jnp.clip(shift.astype(jnp.int32), -HALO, HALO)
            total = load_total(proj, q, EXT)
            project_block(vols, slot, mag, offset, shift, image_1 if q else image_0, total)
            store_total(proj, q, total)

    own_block.wait()
    own_table.wait()
    gather.run(project, between)

    exchange = [
        pair_copy(proj.at[1], other, 1),
        slab_copy(proj.at[0, :, pl.ds(ROWS, 8)], below.at[0], 2, 1),
        slab_copy(proj.at[0, :, pl.ds(0, 8)], above.at[0], 3, SLABS - 1),
        slab_copy(proj.at[1, :, pl.ds(ROWS, 8)], below.at[1], 4, 1, pair),
        slab_copy(proj.at[1, :, pl.ds(0, 8)], above.at[1], 5, SLABS - 1, pair),
    ]
    for copy in exchange:
        copy.start()
    for q in range(2):
        for t in range(TILES):
            column = jnp.zeros((1, 128), jnp.float32)
            for g in range(EXT // 8):
                value = proj[q, t, 8 * g : 8 * g + 8, :]
                if g == 0:
                    value = jnp.where(row + slab * ROWS >= HALO, value, 0.0)
                if g == EXT // 8 - 1:
                    value = jnp.where((row < HALO) | (slab < SLABS - 1), value, 0.0)
                column = column + jnp.sum(value, axis=0, keepdims=True)
            own_sums[q, t : t + 1, :] = column
            if q == 0:
                column = jnp.sum(seen[t, 8 : 8 + ROWS, :], axis=0, keepdims=True)
            else:
                column = jnp.zeros((1, 128), jnp.float32)
            own_sums[q, TILES + t : TILES + t + 1, :] = column
        for j in range(1 - q, SLABS):
            n = 5 + j + 7 * q + q
            if j == 0:
                copy = pair_copy(own_sums.at[1], sums.at[SLABS], 2)
            else:
                copy = slab_copy(own_sums.at[q], sums.at[SLABS * q + j], n, j, pair if q else band)
            copy.start()
            exchange.append(copy)
    fill_pair()
    for copy in [seen_up, seen_down] + exchange:
        copy.wait_recv()

    all_sums = own_sums[0]
    for j in range(1, 2 * SLABS):
        all_sums = all_sums + sums[j]
    for t in range(TILES):
        gain = all_sums[TILES + t : TILES + t + 1, :] / all_sums[t : t + 1, :]
        gain = jnp.broadcast_to(gain, (8, 128))
        for g in range(EXT // 8):
            value = proj[0, t, 8 * g : 8 * g + 8, :] + other[t, 8 * g : 8 * g + 8, :]
            if g == 0:
                value = value + jnp.where(slab > 0, below[0, t] + below[1, t], 0.0)
            if g == EXT // 8 - 1:
                value = value + jnp.where(slab < SLABS - 1, above[0, t] + above[1, t], 0.0)
            value = (seen[t, 8 * g + HALO : 8 * g + HALO + 8, :] - gain * value) * (1.0 / BANDS)
            if g == 0:
                value = jnp.where(row + slab * ROWS >= HALO, value, 0.0)
            if g == EXT // 8 - 1:
                value = jnp.where((row < HALO) | (slab < SLABS - 1), value, 0.0)
            ext[t, 8 * g : 8 * g + 8, :] = value
    double = 2 * (lane & 63)
    for k in range(2):
        for phase in range(2):
            for g in range(EXT // 8):
                a = take(ext[2 * k, 8 * g : 8 * g + 8, :], double + phase)
                b = take(ext[2 * k + 1, 8 * g : 8 * g + 8, :], double + phase)
                first = 2 * EXT * k + EXT * phase + 8 * g
                ress[0, first : first + 8, :] = jnp.where(lane < 64, a, b)

    spread_out = Gather(ress, RES_PARTS, res_send, res_recv, place)
    spread_out.start()
    for t in range(TILES):
        residual_ref[0, :, 128 * t : 128 * (t + 1)] = ext[t, HALO : HALO + ROWS, :]

    def backproject(slot):
        angle = half * COLUMN + order[slot]
        for n in range(0, RES_ROWS, 8):
            rows[n : n + 8, :] = ress[slot, n : n + 8, :]
        for q in range(2):
            shift = pair_ref[2, angle].astype(jnp.int32) if q else shift_ref[angle]
            total = load_total(back, q, ROWS)
            backproject_block(2 * slot + q, jnp.clip(shift, -HALO, HALO), index_ref, weight_ref, rows, total)
            store_total(back, q, total)

    spread_out.run(backproject, lambda: None)
    last = pair_copy(back.at[1], other_back, 3)
    last.start()
    last.wait_recv()
    for t in range(TILES):
        value = (back[0, t] + other_back[t]) * (1.0 / math.sqrt(BANDS))
        correction_ref[0, :, 128 * t : 128 * (t + 1)] = value
    gather.finish()
    spread_out.finish()
    for copy in [pair_values, *values, seen_up, seen_down, last, *exchange]:
        copy.wait_send()


def shards(volume, measured, magnification, shift_y, shift_z):
    hbm, vmem = pl.BlockSpec(memory_space=pltpu.HBM), pl.BlockSpec(memory_space=pltpu.VMEM)
    block = jax.ShapeDtypeStruct(volume.shape, jnp.float32)
    f32 = jnp.float32
    return pl.pallas_call(
        kernel,
        out_shape=(block, block),
        in_specs=[hbm] * 5,
        out_specs=(vmem, vmem),
        scratch_shapes=[
            pltpu.SMEM((BANDS,), f32),
            pltpu.SMEM((BANDS,), jnp.int32),
            pltpu.SMEM((BANDS,), jnp.int32),
            pltpu.SMEM((COLUMN,), jnp.int32),
            pltpu.VMEM((COLUMN, ROWS, 128 * TILES), f32),
            pltpu.VMEM((COLUMN, RES_ROWS, 128), f32),
            pltpu.VMEM((COLUMN, 8, 128), f32),
            pltpu.SMEM((COLUMN, 8, 128), f32),
            pltpu.VMEM((8, 128), f32),
            pltpu.SMEM((8, 128), f32),
            pltpu.VMEM((TILES, ROWS + 16, 128), f32),
            pltpu.VMEM((2, TILES, EXT, 128), f32),
            pltpu.VMEM((TILES, EXT, 128), f32),
            pltpu.VMEM((TILES, EXT, 128), f32),
            pltpu.VMEM((2, TILES, ROWS, 128), f32),
            pltpu.VMEM((TILES, ROWS, 128), f32),
            pltpu.VMEM((2, 8, 128), f32),
            pltpu.VMEM((2 * SLABS, 8, 128), f32),
            pltpu.VMEM((2, TILES, 8, 128), f32),
            pltpu.VMEM((2, TILES, 8, 128), f32),
            pltpu.VMEM((BANDS, 128, 128), jnp.int32),
            pltpu.VMEM((BANDS, 128, 128), f32),
            pltpu.VMEM((TILES, ROWS + 16, 128), f32),
            pltpu.VMEM((TILES, ROWS + 16, 128), f32),
            pltpu.VMEM((RES_ROWS, 128), f32),
            pltpu.SemaphoreType.DMA((COPIES,)),
            pltpu.SemaphoreType.DMA((COPIES,)),
            pltpu.SemaphoreType.DMA((COPIES,)),
            pltpu.SemaphoreType.DMA((COPIES,)),
            pltpu.SemaphoreType.DMA((2 * SLABS + 5,)),
            pltpu.SemaphoreType.DMA((2 * SLABS + 5,)),
            pltpu.SemaphoreType.DMA((4,)),
            pltpu.SemaphoreType.DMA((4,)),
            pltpu.SemaphoreType.DMA((COLUMN,)),
            pltpu.SemaphoreType.DMA((COLUMN,)),
            pltpu.SemaphoreType.DMA((4 + TILES,)),
        ],
        compiler_params=pltpu.CompilerParams(
            collective_id=0, has_side_effects=True, vmem_limit_bytes=62 * 1024 * 1024
        ),
        name="sirt",
    )(
        magnification.reshape(BANDS),
        shift_y.reshape(BANDS),
        shift_z.reshape(BANDS),
        volume,
        measured,
    )


def solution(mesh):
    return jax.shard_map(
        shards,
        mesh=mesh,
        in_specs=(
            P("xband", "zslab", None),
            P("xband", "zslab", None),
            P(None, "xband"),
            P(None, "xband"),
            P(None, "xband"),
        ),
        out_specs=(P("xband", "zslab", None), P("xband", "zslab", None)),
        check_vma=False,
    )
```

```python
import functools
import math

import jax
import jax.numpy as jnp
from jax import lax
from jax.experimental import pallas as pl
from jax.experimental.pallas import tpu as pltpu
from jax.sharding import PartitionSpec as P

HALO = 4
TILES = 4
ROWS = 32
EXT = ROWS + 2 * HALO
SLABS = 8
RING = 8
BANDS = 32
CENTRE = 255.5
RES_ROWS = TILES * ROWS
VOL_PARTS = ((0, 16), (16, 16), (0, 32))
RES_PARTS = ((0, 64), (64, 64), (0, 128))
COPIES = 20
COLUMN = 16
FORWARD_TILES = ((0, 1), (0, 1, 2), (1, 2, 3), (2, 3))
BACKWARD_TILES = ((0,), (0, 1), (0, 1), (1,))
MESH = pl.DeviceIdType.MESH


def take(x, index):
    return jnp.take_along_axis(x, index, axis=1, mode="promise_in_bounds")


def iota(axis):
    return lax.broadcasted_iota(jnp.int32, (8, 128), axis)


def take_tiles(tiles, index):
    lanes = index & 127
    values = None
    for k, groups in tiles.items():
        part = [take(x, lanes) for x in groups]
        if values is None:
            values = part
        else:
            here = index >= 128 * k
            values = [jnp.where(here, p, v) for p, v in zip(part, values)]
    return values


def moved(work, tile, shift, total):
    return [t + work[tile, pl.ds(8 + 8 * g - HALO - shift, 8), :] for g, t in enumerate(total)]


def project_tile(blocks, slot, ub, mag, offset, shift, work, total):
    mag = jnp.full((8, 128), mag, jnp.float32)
    u = (iota(1) + 128 * ub).astype(jnp.float32)
    target = (u - CENTRE) / mag + CENTRE + offset
    lower = jnp.floor(target)
    frac = target - lower
    left = lower.astype(jnp.int32)
    tiles = {
        k: [blocks[slot, 8 * g : 8 * g + 8, 128 * k : 128 * k + 128] for g in range(ROWS // 8)]
        for k in FORWARD_TILES[ub]
    }
    a = take_tiles(tiles, left)
    b = take_tiles(tiles, left + 1)
    for g in range(ROWS // 8):
        work[ub, 8 + 8 * g : 16 + 8 * g, :] = (1.0 - frac) * a[g] + frac * b[g]
    return moved(work, ub, shift, total)


def tap_tables(mag, offset, index_ref, weight_ref, angle):
    lane = iota(1)
    mag = jnp.full((8, 128), mag, jnp.float32)
    for yb in range(TILES):
        y = (lane + 128 * yb).astype(jnp.float32)
        middle = (y - CENTRE - offset) * mag + CENTRE
        for phase in range(2):
            first = jnp.floor((middle - phase) * 0.5).astype(jnp.int32)
            for tap in range(2):
                j = first + tap
                u = (2 * j + phase).astype(jnp.float32)
                target = (u - CENTRE) / mag + CENTRE + offset
                weight = jnp.maximum(0.0, 1.0 - jnp.abs(y - target))
                weight = jnp.where((j >= 0) & (j < 256), weight, 0.0)
                n = 8 * (yb * 4 + phase * 2 + tap)
                index_ref[angle, n : n + 8, :] = jnp.clip(j, 0, 255)
                weight_ref[angle, n : n + 8, :] = weight


def backproject_tile(blocks, slot, yb, angle, shift, index_ref, weight_ref, work, total):
    image = [jnp.zeros((8, 128), jnp.float32)] * (ROWS // 8)
    for phase in range(2):
        tiles = {}
        for k in BACKWARD_TILES[yb]:
            start = ROWS * (2 * k + phase)
            tiles[k] = [blocks[slot, start + 8 * g : start + 8 * g + 8, :] for g in range(ROWS // 8)]
        for tap in range(2):
            n = 8 * (4 * yb + 2 * phase + tap)
            values = take_tiles(tiles, index_ref[angle, n : n + 8, :])
            weight = weight_ref[angle, n : n + 8, :]
            image = [i + weight * v for i, v in zip(image, values)]
    for g, value in enumerate(image):
        work[yb, 8 + 8 * g : 16 + 8 * g, :] = value
    return moved(work, yb, -shift, total)


OWN = (0, 2, 3, 4, 5, 10, 11, 12)
OTHER = (1, 6, 7, 8, 9, 13, 14, 15)
AWAY = (0, 1, -1, 2, -2, 3, -3, 4)


class Gather:
    def __init__(self, blocks, parts, send, recv, place, own=None):
        self.blocks, self.parts, self.send_sem, self.recv_sem = blocks, parts, send, recv
        self.place = place
        self.own = blocks.at[0] if own is None else own
        self.sent = []

    def copy(self, source, target, part, n, to):
        rows = pl.ds(*self.parts[part])
        return pltpu.make_async_remote_copy(
            src_ref=source.at[rows],
            dst_ref=self.blocks.at[target, rows],
            send_sem=self.send_sem.at[n],
            recv_sem=self.recv_sem.at[n],
            device_id={"xband": self.place[to]},
            device_id_type=MESH,
        )

    def send(self, source, target, part, n, to):
        self.copy(self.blocks.at[source] if source else self.own, target, part, n, to).start()
        self.sent.append((source, target, part, n, to))

    def wait(self, slot, part, n):
        self.copy(self.blocks.at[slot], slot, part, n, "core").wait_recv()

    def start(self):
        for part in range(2):
            self.send(0, OWN[3], part, 2 + part, "long2")
            self.send(0, OWN[4], part, 4 + part, "short2")
        self.send(0, OWN[1], 2, 0, "long1")
        self.send(0, OWN[2], 2, 1, "short1")
        self.core(0)

    def core(self, p):
        self.send(OWN[p], OTHER[p], 2, 12 + p, "core")

    def from_core(self, p):
        self.wait(OTHER[p], 2, 12 + p)

    def run(self, compute, finish, hooks=None):
        hooks = hooks or {}
        def first():
            if "first" in hooks:
                hooks["first"]()
            for part in range(2):
                self.wait(OWN[3], part, 2 + part)
                self.send(OWN[3], OWN[7], part, 8 + part, "long2")
                self.send(OWN[3], OWN[5], part, 6 + part, "long1")
                self.wait(OWN[4], part, 4 + part)
                self.send(OWN[4], OWN[6], part, 10 + part, "short1")
                if "far" in hooks and part == 0:
                    hooks["far"]()
            self.core(3)
            self.core(4)
            for n, p in enumerate((1, 2)):
                self.wait(OWN[p], 2, n)
                self.core(p)
            self.from_core(0)

        def last():
            for p, n in ((5, 6), (6, 10), (7, 8)):
                self.wait(OWN[p], 0, n)
                self.wait(OWN[p], 1, n + 1)
                self.core(p)

        actions = {1: first, OWN[5]: last}
        for p in range(1, RING - 1):
            actions[OTHER[p]] = functools.partial(self.from_core, p)

        def one(slot, carry):
            for n, action in actions.items():
                pl.when(slot == n)(action)
                if n in hooks:
                    pl.when(slot == n)(hooks[n])
            compute(slot)
            return carry

        lax.fori_loop(0, COLUMN - 1, one, 0)
        self.from_core(RING - 1)
        finish(COLUMN - 1)

    def finish(self):
        for source, *rest in self.sent:
            self.copy(self.blocks.at[source] if source else self.own, *rest).wait_send()


def load_total(ref, q, t):
    return [ref[q, t, 8 * g : 8 * g + 8, :] for g in range(EXT // 8)]


def store_total(ref, q, t, total):
    for g, value in enumerate(total):
        ref[q, t, 8 * g : 8 * g + 8, :] = value


def kernel(
    mag_hbm, offset_hbm, shift_hbm, volume_ref, measured_ref, residual_ref, correction_ref,
    mag_ref, offset_ref, shift_ref, order,
    vols, ress, tables_vmem, tables, pair_vmem, pair_ref, seen, proj, back, other, ext, own_sums, sums,
    below, above, index_ref, weight_ref, image_0, image_1,
    vol_send, vol_recv, res_send, res_recv, slab_send, slab_recv, pair_send, pair_recv,
    values_send, values_recv, local_sem, word_sem,
):
    slab, band = lax.axis_index("zslab"), lax.axis_index("xband")
    half, core = lax.div(band, 16), lax.rem(band, 2)
    z = lax.div(lax.rem(band, 16), 2)
    turn = 1 - 2 * core
    pair = (1 - half) * COLUMN + lax.rem(band, COLUMN)

    def ring(away, core=core):
        return half * COLUMN + lax.rem(z + away + 2 * RING, RING) * 2 + core

    scalars = [
        pltpu.make_async_copy(source, target, local_sem.at[n])
        for n, (source, target) in enumerate(
            ((mag_hbm, mag_ref), (offset_hbm, offset_ref), (shift_hbm, shift_ref))
        )
    ]
    own_block = pltpu.make_async_copy(volume_ref.at[0], vols.at[0], local_sem.at[3])
    own_seen = pltpu.make_async_copy(measured_ref.at[0], seen, local_sem.at[4])
    for copy in [*scalars, own_block, own_seen]:
        copy.start()

    place = {
        "long1": ring(turn),
        "long2": ring(2 * turn),
        "short1": ring(-turn),
        "short2": ring(-2 * turn),
        "core": band + turn,
        "pair": pair,
    }
    for p, away in enumerate(AWAY):
        order[OWN[p]] = lax.rem(z - turn * away + 2 * RING, RING) * 2 + core
        order[OTHER[p]] = lax.rem(z + turn * away + 2 * RING, RING) * 2 + 1 - core
    barrier = pltpu.get_barrier_semaphore()
    for to in place.values():
        pl.semaphore_signal(barrier, inc=1, device_id={"xband": to}, device_id_type=MESH)
    slabs = [lax.rem(slab + j, SLABS) for j in range(SLABS)]
    for to in (slabs[1], slabs[SLABS - 1]):
        for of in (band, pair):
            pl.semaphore_signal(barrier, inc=1, device_id={"zslab": to, "xband": of}, device_id_type=MESH)

    pl.semaphore_wait(barrier, len(place) + 4)

    gather = Gather(vols, VOL_PARTS, vol_send, vol_recv, place, volume_ref.at[0])
    gather.start()

    lane, row = iota(1), iota(0)
    for copy in scalars:
        copy.wait()

    def spread(angle, values):
        here = lane == angle
        mags, offsets, shifts = values
        return (
            jnp.where(here, mag_ref[angle], mags),
            jnp.where(here, offset_ref[angle].astype(jnp.float32), offsets),
            jnp.where(here, shift_ref[angle].astype(jnp.float32), shifts),
        )

    zeros = jnp.zeros((8, 128), jnp.float32)
    mags, offsets, shifts = lax.fori_loop(0, BANDS, spread, (zeros, zeros, zeros))
    tables_vmem[0] = jnp.where(row == 0, mags, jnp.where(row == 1, offsets, shifts))

    def tell(n):
        for side, to in enumerate((slabs[n + 1], slabs[SLABS - 1 - n])):
            pl.semaphore_signal(word_sem.at[n, side], inc=1, device_id={"zslab": to}, device_id_type=MESH)

    def hear(n):
        for side in range(2):
            pl.semaphore_wait(word_sem.at[n, side], 1)

    tell(0)

    def pair_copy(source, target, n):
        return pltpu.make_async_remote_copy(
            src_ref=source,
            dst_ref=target,
            send_sem=pair_send.at[n],
            recv_sem=pair_recv.at[n],
            device_id={"xband": pair},
            device_id_type=MESH,
        )

    def slab_copy(source, target, n, to, of=band):
        return pltpu.make_async_remote_copy(
            src_ref=source,
            dst_ref=target,
            send_sem=slab_send.at[n],
            recv_sem=slab_recv.at[n],
            device_id={"zslab": slabs[to], "xband": of},
            device_id_type=MESH,
        )

    pair_values = pair_copy(tables_vmem.at[0], pair_vmem, 0)
    pair_values.start()
    def values_copy(source, target, to):
        return pltpu.make_async_remote_copy(
            src_ref=tables_vmem.at[source],
            dst_ref=tables_vmem.at[target],
            send_sem=values_send.at[target],
            recv_sem=values_recv.at[target],
            device_id={"xband": place[to]},
            device_id_type=MESH,
        )

    routes = (
        (0, OWN[3], "long2"), (0, OWN[4], "short2"), (0, OWN[1], "long1"), (0, OWN[2], "short1"),
        (OWN[3], OWN[7], "long2"), (OWN[3], OWN[5], "long1"), (OWN[4], OWN[6], "short1"),
        *((OWN[p], OTHER[p], "core") for p in range(RING)),
    )
    for route in (*routes[:4], routes[7]):
        values_copy(*route).start()

    def values_on(p):
        values_copy(0, OWN[p], "core").wait_recv()
        for route in routes:
            if route[0] == OWN[p]:
                values_copy(*route).start()

    def to_smem(first, count, n):
        rows = pl.ds(first, count)
        return pltpu.make_async_copy(tables_vmem.at[rows], tables.at[rows], local_sem.at[n])

    own_table = pltpu.make_async_copy(tables_vmem.at[0], tables.at[0], local_sem.at[0])
    own_table.start()
    for t in range(TILES):
        for image in (image_0, image_1):
            image[t, 0:8, :] = zeros
            image[t, 8 + ROWS :, :] = zeros
        for q in range(2):
            proj[q, t] = jnp.zeros((EXT, 128), jnp.float32)
            back[q, t] = jnp.zeros((EXT, 128), jnp.float32)

    def fill_own(n, carry):
        angle = half * COLUMN + order[n]
        tap_tables(mag_ref[angle], offset_ref[angle].astype(jnp.float32), index_ref, weight_ref, 2 * n)
        return carry

    lax.fori_loop(0, COLUMN, fill_own, 0)

    def near_values():
        pair_values.wait_recv()
        local = pltpu.make_async_copy(pair_vmem, pair_ref, local_sem.at[1])
        local.start()
        for p in (1, 2):
            values_on(p)
        values_copy(0, OTHER[0], "core").wait_recv()
        near = to_smem(1, 5, 2)
        near.start()
        near.wait()
        local.wait()

    def core_values():
        for p in range(1, 5):
            values_copy(0, OTHER[p], "core").wait_recv()
        core = to_smem(OTHER[1], 4, 2)
        core.start()
        core.wait()

    def far_values():
        for p in (5, 6, 7):
            values_on(p)

    def last_values():
        for p in (5, 6, 7):
            values_copy(0, OTHER[p], "core").wait_recv()
        far = to_smem(OWN[5], 6, 2)
        far.start()
        far.wait()

    def fill_pair():
        def one(n, carry):
            angle = half * COLUMN + order[n]
            tap_tables(pair_ref[0, angle], pair_ref[1, angle], index_ref, weight_ref, 2 * n + 1)
            return carry

        lax.fori_loop(0, COLUMN, one, 0)

    images = (image_0, image_1)
    exchanged = []

    def start(copy):
        copy.start()
        exchanged.append(copy)

    def tiles_apart(ref, tile, phase, after):
        def finish(slot):
            for q in (1, 0):
                values = tile(slot, q)
                for t in range(TILES):
                    store_total(ref, q, t, values(t, load_total(ref, q, t)))
                    if q:
                        start(pair_copy(ref.at[1, t], other.at[phase, t], 2 + TILES * phase + t))
                of, n = (pair, 4 * phase + 2) if q else (band, 4 * phase)
                start(slab_copy(ref.at[q, :, pl.ds(ROWS, 8)], below.at[phase, q], n, 1, of))
                start(slab_copy(ref.at[q, :, pl.ds(0, 8)], above.at[phase, q], n + 1, SLABS - 1, of))
                after(q)

        return finish

    def each(ref, tile):
        def compute(slot):
            for q in range(2):
                values = tile(slot, q)
                for t in range(TILES):
                    store_total(ref, q, t, values(t, load_total(ref, q, t)))

        return compute

    def full_rows(ref, t, phase):
        for g in range(EXT // 8):
            value = ref[0, t, 8 * g : 8 * g + 8, :] + other[phase, t, 8 * g : 8 * g + 8, :]
            if g == 0:
                value = value + jnp.where(slab > 0, below[phase, 0, t] + below[phase, 1, t], 0.0)
            if g == EXT // 8 - 1:
                value = value + jnp.where(slab < SLABS - 1, above[phase, 0, t] + above[phase, 1, t], 0.0)
            ext[t, 8 * g : 8 * g + 8, :] = value

    def project(slot, q):
        angle = pair if q else band
        mag, offset, shift = (tables[slot, n, angle] for n in range(3))
        shift = jnp.clip(shift.astype(jnp.int32), -HALO, HALO)
        return lambda t, total: project_tile(vols, slot, t, mag, offset, shift, images[q], total)

    def send_sums(q):
        for t in range(TILES):
            column = jnp.zeros((1, 128), jnp.float32)
            for g in range(EXT // 8):
                value = proj[q, t, 8 * g : 8 * g + 8, :]
                if g == 0:
                    value = jnp.where(row + slab * ROWS >= HALO, value, 0.0)
                if g == EXT // 8 - 1:
                    value = jnp.where((row < HALO) | (slab < SLABS - 1), value, 0.0)
                column = column + jnp.sum(value, axis=0, keepdims=True)
            own_sums[q, t : t + 1, :] = column
        if q:
            start(pair_copy(own_sums.at[1], sums.at[SLABS], 1))
        for j in range(1, SLABS):
            start(slab_copy(own_sums.at[q], sums.at[SLABS * q + j], 7 + 7 * q + j, j, pair if q else band))

    own_seen.wait()
    for t in range(TILES):
        column = jnp.sum(seen[:, 128 * t : 128 * t + 128], axis=0, keepdims=True)
        own_sums[0, TILES + t : TILES + t + 1, :] = column
        own_sums[1, TILES + t : TILES + t + 1, :] = jnp.zeros((1, 128), jnp.float32)
    own_block.wait()
    own_table.wait()
    hooks = {
        "first": lambda: [hear(0), tell(1)],
        "far": lambda: [values_on(3), values_on(4)],
        1: near_values,
        6: core_values,
        7: lambda: hear(1),
        8: far_values,
        9: last_values,
    }
    gather.run(each(proj, project), tiles_apart(proj, project, 0, send_sums), hooks)
    fill_pair()
    for copy in exchanged:
        copy.wait_recv()

    all_sums = own_sums[0]
    for j in range(1, 2 * SLABS):
        all_sums = all_sums + sums[j]
    for t in range(TILES):
        full_rows(proj, t, 0)
        gain = all_sums[TILES + t : TILES + t + 1, :] / all_sums[t : t + 1, :]
        gain = jnp.broadcast_to(gain, (8, 128))
        for g in range(ROWS // 8):
            value = seen[8 * g : 8 * g + 8, 128 * t : 128 * t + 128]
            value = value - gain * ext[t, HALO + 8 * g : HALO + 8 * g + 8, :]
            residual_ref[0, 8 * g : 8 * g + 8, 128 * t : 128 * t + 128] = value
    double = 2 * (lane & 63)
    for k in range(2):
        for phase in range(2):
            for g in range(ROWS // 8):
                a = residual_ref[0, 8 * g : 8 * g + 8, 256 * k : 256 * k + 128]
                b = residual_ref[0, 8 * g : 8 * g + 8, 256 * k + 128 : 256 * k + 256]
                first = ROWS * (2 * k + phase) + 8 * g
                value = jnp.where(lane < 64, take(a, double + phase), take(b, double + phase))
                ress[0, first : first + 8, :] = value

    spread_out = Gather(ress, RES_PARTS, res_send, res_recv, place)
    spread_out.start()

    def backproject(slot, q):
        angle = half * COLUMN + order[slot]
        shift = pair_ref[2, angle].astype(jnp.int32) if q else shift_ref[angle]
        shift = jnp.clip(shift, -HALO, HALO)
        return lambda t, total: backproject_tile(
            ress, slot, t, 2 * slot + q, shift, index_ref, weight_ref, images[q], total
        )

    before = len(exchanged)
    spread_out.run(each(back, backproject), tiles_apart(back, backproject, 1, lambda q: None))
    for copy in exchanged[before:]:
        copy.wait_recv()
    for t in range(TILES):
        full_rows(back, t, 1)
        correction_ref[0, :, 128 * t : 128 * (t + 1)] = ext[t, HALO : HALO + ROWS, :]
    gather.finish()
    spread_out.finish()
    for route in routes:
        values_copy(*route).wait_send()
    for copy in [pair_values, *exchanged]:
        copy.wait_send()


def shards(volume, measured, magnification, shift_y, shift_z):
    hbm, vmem = pl.BlockSpec(memory_space=pltpu.HBM), pl.BlockSpec(memory_space=pltpu.VMEM)
    block = jax.ShapeDtypeStruct(volume.shape, jnp.float32)
    f32 = jnp.float32
    residual, correction = pl.pallas_call(
        kernel,
        out_shape=(block, block),
        in_specs=[hbm] * 5,
        out_specs=(vmem, vmem),
        scratch_shapes=[
            pltpu.SMEM((BANDS,), f32),
            pltpu.SMEM((BANDS,), jnp.int32),
            pltpu.SMEM((BANDS,), jnp.int32),
            pltpu.SMEM((COLUMN,), jnp.int32),
            pltpu.VMEM((COLUMN, ROWS, 128 * TILES), f32),
            pltpu.VMEM((COLUMN, RES_ROWS, 128), f32),
            pltpu.VMEM((COLUMN, 8, 128), f32),
            pltpu.SMEM((COLUMN, 8, 128), f32),
            pltpu.VMEM((8, 128), f32),
            pltpu.SMEM((8, 128), f32),
            pltpu.VMEM((ROWS, 128 * TILES), f32),
            pltpu.VMEM((2, TILES, EXT, 128), f32),
            pltpu.VMEM((2, TILES, EXT, 128), f32),
            pltpu.VMEM((2, TILES, EXT, 128), f32),
            pltpu.VMEM((TILES, EXT, 128), f32),
            pltpu.VMEM((2, 8, 128), f32),
            pltpu.VMEM((2 * SLABS, 8, 128), f32),
            pltpu.VMEM((2, 2, TILES, 8, 128), f32),
            pltpu.VMEM((2, 2, TILES, 8, 128), f32),
            pltpu.VMEM((BANDS, 128, 128), jnp.int32),
            pltpu.VMEM((BANDS, 128, 128), f32),
            pltpu.VMEM((TILES, ROWS + 16, 128), f32),
            pltpu.VMEM((TILES, ROWS + 16, 128), f32),
            pltpu.SemaphoreType.DMA((COPIES,)),
            pltpu.SemaphoreType.DMA((COPIES,)),
            pltpu.SemaphoreType.DMA((COPIES,)),
            pltpu.SemaphoreType.DMA((COPIES,)),
            pltpu.SemaphoreType.DMA((22,)),
            pltpu.SemaphoreType.DMA((22,)),
            pltpu.SemaphoreType.DMA((2 + 2 * TILES,)),
            pltpu.SemaphoreType.DMA((2 + 2 * TILES,)),
            pltpu.SemaphoreType.DMA((COLUMN,)),
            pltpu.SemaphoreType.DMA((COLUMN,)),
            pltpu.SemaphoreType.DMA((5,)),
            pltpu.SemaphoreType.REGULAR((2, 2)),
        ],
        compiler_params=pltpu.CompilerParams(
            collective_id=0, has_side_effects=True, vmem_limit_bytes=55040 * 1024
        ),
        name="sirt",
    )(
        magnification.reshape(BANDS),
        shift_y.reshape(BANDS),
        shift_z.reshape(BANDS),
        volume,
        measured,
    )
    return residual * (1.0 / BANDS), correction * (1.0 / (BANDS * math.sqrt(BANDS)))


def solution(mesh):
    return jax.shard_map(
        shards,
        mesh=mesh,
        in_specs=(
            P("xband", "zslab", None),
            P("xband", "zslab", None),
            P(None, "xband"),
            P(None, "xband"),
            P(None, "xband"),
        ),
        out_specs=(P("xband", "zslab", None), P("xband", "zslab", None)),
        check_vma=False,
    )
```

```python
import functools
import math

import jax
import jax.numpy as jnp
from jax import lax
from jax.experimental import pallas as pl
from jax.experimental.pallas import tpu as pltpu
from jax.sharding import PartitionSpec as P

HALO = 4
TILES = 4
ROWS = 32
EXT = ROWS + 2 * HALO
SLABS = 8
RING = 8
BANDS = 32
CENTRE = 255.5
RES_ROWS = TILES * ROWS
VOL_PARTS = ((0, 16), (16, 16), (0, 32))
RES_PARTS = ((0, 64), (64, 64), (0, 128))
COPIES = 20
COLUMN = 16
FORWARD_TILES = ((0, 1), (0, 1, 2), (1, 2, 3), (2, 3))
BACKWARD_TILES = ((0,), (0, 1), (0, 1), (1,))
MESH = pl.DeviceIdType.MESH


def take(x, index):
    return jnp.take_along_axis(x, index, axis=1, mode="promise_in_bounds")


def iota(axis):
    return lax.broadcasted_iota(jnp.int32, (8, 128), axis)


def take_tiles(tiles, index):
    lanes = index & 127
    values = None
    for k, groups in tiles.items():
        part = [take(x, lanes) for x in groups]
        if values is None:
            values = part
        else:
            here = index >= 128 * k
            values = [jnp.where(here, p, v) for p, v in zip(part, values)]
    return values


def moved(work, tile, shift, total):
    return [t + work[tile, pl.ds(8 + 8 * g - HALO - shift, 8), :] for g, t in enumerate(total)]


def project_tile(blocks, slot, ub, mag, offset, shift, work, total):
    mag = jnp.full((8, 128), mag, jnp.float32)
    u = (iota(1) + 128 * ub).astype(jnp.float32)
    target = (u - CENTRE) / mag + CENTRE + offset
    lower = jnp.floor(target)
    frac = target - lower
    left = lower.astype(jnp.int32)
    tiles = {
        k: [blocks[slot, 8 * g : 8 * g + 8, 128 * k : 128 * k + 128] for g in range(ROWS // 8)]
        for k in FORWARD_TILES[ub]
    }
    a = take_tiles(tiles, left)
    b = take_tiles(tiles, left + 1)
    for g in range(ROWS // 8):
        work[ub, 8 + 8 * g : 16 + 8 * g, :] = (1.0 - frac) * a[g] + frac * b[g]
    return moved(work, ub, shift, total)


def tap_tables(mag, offset, index_ref, weight_ref, angle):
    lane = iota(1)
    mag = jnp.full((8, 128), mag, jnp.float32)
    for yb in range(TILES):
        y = (lane + 128 * yb).astype(jnp.float32)
        middle = (y - CENTRE - offset) * mag + CENTRE
        for phase in range(2):
            first = jnp.floor((middle - phase) * 0.5).astype(jnp.int32)
            for tap in range(2):
                j = first + tap
                u = (2 * j + phase).astype(jnp.float32)
                target = (u - CENTRE) / mag + CENTRE + offset
                weight = jnp.maximum(0.0, 1.0 - jnp.abs(y - target))
                weight = jnp.where((j >= 0) & (j < 256), weight, 0.0)
                n = 8 * (yb * 4 + phase * 2 + tap)
                index_ref[angle, n : n + 8, :] = jnp.clip(j, 0, 255)
                weight_ref[angle, n : n + 8, :] = weight


def backproject_tile(blocks, slot, yb, angle, shift, index_ref, weight_ref, work, total):
    image = [jnp.zeros((8, 128), jnp.float32)] * (ROWS // 8)
    for phase in range(2):
        tiles = {}
        for k in BACKWARD_TILES[yb]:
            start = ROWS * (2 * k + phase)
            tiles[k] = [blocks[slot, start + 8 * g : start + 8 * g + 8, :] for g in range(ROWS // 8)]
        for tap in range(2):
            n = 8 * (4 * yb + 2 * phase + tap)
            values = take_tiles(tiles, index_ref[angle, n : n + 8, :])
            weight = weight_ref[angle, n : n + 8, :]
            image = [i + weight * v for i, v in zip(image, values)]
    for g, value in enumerate(image):
        work[yb, 8 + 8 * g : 16 + 8 * g, :] = value
    return moved(work, yb, -shift, total)


OWN = (0, 2, 3, 4, 5, 10, 11, 12)
OTHER = (1, 6, 7, 8, 9, 13, 14, 15)
AWAY = (0, 1, -1, 2, -2, 3, -3, 4)


class Gather:
    def __init__(self, blocks, parts, send, recv, place, own=None):
        self.blocks, self.parts, self.send_sem, self.recv_sem = blocks, parts, send, recv
        self.place = place
        self.own = blocks.at[0] if own is None else own
        self.sent = []

    def copy(self, source, target, part, n, to):
        rows = pl.ds(*self.parts[part])
        return pltpu.make_async_remote_copy(
            src_ref=source.at[rows],
            dst_ref=self.blocks.at[target, rows],
            send_sem=self.send_sem.at[n],
            recv_sem=self.recv_sem.at[n],
            device_id={"xband": self.place[to]},
            device_id_type=MESH,
        )

    def send(self, source, target, part, n, to):
        self.copy(self.blocks.at[source] if source else self.own, target, part, n, to).start()
        self.sent.append((source, target, part, n, to))

    def wait(self, slot, part, n):
        self.copy(self.blocks.at[slot], slot, part, n, "core").wait_recv()

    def start(self):
        for part in range(2):
            self.send(0, OWN[3], part, 2 + part, "long2")
            self.send(0, OWN[4], part, 4 + part, "short2")
        self.send(0, OWN[1], 2, 0, "long1")
        self.send(0, OWN[2], 2, 1, "short1")
        self.core(0)

    def core(self, p):
        self.send(OWN[p], OTHER[p], 2, 12 + p, "core")

    def from_core(self, p):
        self.wait(OTHER[p], 2, 12 + p)

    def run(self, compute, finish, hooks=None):
        hooks = hooks or {}
        def first():
            if "first" in hooks:
                hooks["first"]()
            for part in range(2):
                self.wait(OWN[3], part, 2 + part)
                self.send(OWN[3], OWN[7], part, 8 + part, "long2")
                self.send(OWN[3], OWN[5], part, 6 + part, "long1")
                self.wait(OWN[4], part, 4 + part)
                self.send(OWN[4], OWN[6], part, 10 + part, "short1")
                if "far" in hooks and part == 0:
                    hooks["far"]()
            self.core(3)
            self.core(4)
            for n, p in enumerate((1, 2)):
                self.wait(OWN[p], 2, n)
                self.core(p)
            self.from_core(0)

        def last():
            for p, n in ((5, 6), (6, 10), (7, 8)):
                self.wait(OWN[p], 0, n)
                self.wait(OWN[p], 1, n + 1)
                self.core(p)

        actions = {1: first, OWN[5]: last}
        for p in range(1, RING - 1):
            actions[OTHER[p]] = functools.partial(self.from_core, p)

        def one(slot, carry):
            for n, action in actions.items():
                pl.when(slot == n)(action)
                if n in hooks:
                    pl.when(slot == n)(hooks[n])
            compute(slot)
            return carry

        lax.fori_loop(0, COLUMN - 1, one, 0)
        self.from_core(RING - 1)
        finish(COLUMN - 1)

    def finish(self):
        for source, *rest in self.sent:
            self.copy(self.blocks.at[source] if source else self.own, *rest).wait_send()


def load_total(ref, q, t):
    return [ref[q, t, 8 * g : 8 * g + 8, :] for g in range(EXT // 8)]


def store_total(ref, q, t, total):
    for g, value in enumerate(total):
        ref[q, t, 8 * g : 8 * g + 8, :] = value


def kernel(
    mag_hbm, offset_hbm, shift_hbm, volume_ref, measured_ref, residual_ref, correction_ref,
    mag_ref, offset_ref, shift_ref, order,
    vols, ress, tables_vmem, tables, pair_vmem, pair_ref, seen, proj, back, other, ext, own_sums, sums,
    below, above, index_ref, weight_ref, image_0, image_1,
    vol_send, vol_recv, res_send, res_recv, slab_send, slab_recv, pair_send, pair_recv,
    values_send, values_recv, local_sem, word_sem,
):
    slab, band = lax.axis_index("zslab"), lax.axis_index("xband")
    half, core = lax.div(band, 16), lax.rem(band, 2)
    z = lax.div(lax.rem(band, 16), 2)
    turn = 1 - 2 * core
    pair = (1 - half) * COLUMN + lax.rem(band, COLUMN)

    def ring(away, core=core):
        return half * COLUMN + lax.rem(z + away + 2 * RING, RING) * 2 + core

    scalars = [
        pltpu.make_async_copy(source, target, local_sem.at[n])
        for n, (source, target) in enumerate(
            ((mag_hbm, mag_ref), (offset_hbm, offset_ref), (shift_hbm, shift_ref))
        )
    ]
    own_block = pltpu.make_async_copy(volume_ref.at[0], vols.at[0], local_sem.at[3])
    own_seen = pltpu.make_async_copy(measured_ref.at[0], seen, local_sem.at[4])
    for copy in [*scalars, own_block, own_seen]:
        copy.start()

    place = {
        "long1": ring(turn),
        "long2": ring(2 * turn),
        "short1": ring(-turn),
        "short2": ring(-2 * turn),
        "core": band + turn,
        "pair": pair,
    }
    for p, away in enumerate(AWAY):
        order[OWN[p]] = lax.rem(z - turn * away + 2 * RING, RING) * 2 + core
        order[OTHER[p]] = lax.rem(z + turn * away + 2 * RING, RING) * 2 + 1 - core
    barrier = pltpu.get_barrier_semaphore()
    for to in place.values():
        pl.semaphore_signal(barrier, inc=1, device_id={"xband": to}, device_id_type=MESH)
    slabs = [lax.rem(slab + j, SLABS) for j in range(SLABS)]
    for to in (slabs[1], slabs[SLABS - 1]):
        for of in (band, pair):
            pl.semaphore_signal(barrier, inc=1, device_id={"zslab": to, "xband": of}, device_id_type=MESH)

    pl.semaphore_wait(barrier, len(place) + 4)

    gather = Gather(vols, VOL_PARTS, vol_send, vol_recv, place, volume_ref.at[0])
    gather.start()

    lane, row = iota(1), iota(0)
    for copy in scalars:
        copy.wait()

    def spread(angle, values):
        here = lane == angle
        mags, offsets, shifts = values
        return (
            jnp.where(here, mag_ref[angle], mags),
            jnp.where(here, offset_ref[angle].astype(jnp.float32), offsets),
            jnp.where(here, shift_ref[angle].astype(jnp.float32), shifts),
        )

    zeros = jnp.zeros((8, 128), jnp.float32)
    mags, offsets, shifts = lax.fori_loop(0, BANDS, spread, (zeros, zeros, zeros))
    tables_vmem[0] = jnp.where(row == 0, mags, jnp.where(row == 1, offsets, shifts))

    def tell(n):
        for side, to in enumerate((slabs[n + 1], slabs[SLABS - 1 - n])):
            pl.semaphore_signal(word_sem.at[n, side], inc=1, device_id={"zslab": to}, device_id_type=MESH)

    def hear(n):
        for side in range(2):
            pl.semaphore_wait(word_sem.at[n, side], 1)

    tell(0)

    def pair_copy(source, target, n):
        return pltpu.make_async_remote_copy(
            src_ref=source,
            dst_ref=target,
            send_sem=pair_send.at[n],
            recv_sem=pair_recv.at[n],
            device_id={"xband": pair},
            device_id_type=MESH,
        )

    def slab_copy(source, target, n, to, of=band):
        return pltpu.make_async_remote_copy(
            src_ref=source,
            dst_ref=target,
            send_sem=slab_send.at[n],
            recv_sem=slab_recv.at[n],
            device_id={"zslab": slabs[to], "xband": of},
            device_id_type=MESH,
        )

    pair_values = pair_copy(tables_vmem.at[0], pair_vmem, 0)
    pair_values.start()
    def values_copy(source, target, to):
        return pltpu.make_async_remote_copy(
            src_ref=tables_vmem.at[source],
            dst_ref=tables_vmem.at[target],
            send_sem=values_send.at[target],
            recv_sem=values_recv.at[target],
            device_id={"xband": place[to]},
            device_id_type=MESH,
        )

    routes = (
        (0, OWN[3], "long2"), (0, OWN[4], "short2"), (0, OWN[1], "long1"), (0, OWN[2], "short1"),
        (OWN[3], OWN[7], "long2"), (OWN[3], OWN[5], "long1"), (OWN[4], OWN[6], "short1"),
        *((OWN[p], OTHER[p], "core") for p in range(RING)),
    )
    for route in (*routes[:4], routes[7]):
        values_copy(*route).start()

    def values_on(p):
        values_copy(0, OWN[p], "core").wait_recv()
        for route in routes:
            if route[0] == OWN[p]:
                values_copy(*route).start()

    def to_smem(first, count, n):
        rows = pl.ds(first, count)
        return pltpu.make_async_copy(tables_vmem.at[rows], tables.at[rows], local_sem.at[n])

    own_table = pltpu.make_async_copy(tables_vmem.at[0], tables.at[0], local_sem.at[0])
    own_table.start()
    for t in range(TILES):
        for image in (image_0, image_1):
            image[t, 0:8, :] = zeros
            image[t, 8 + ROWS :, :] = zeros
        for q in range(2):
            proj[q, t] = jnp.zeros((EXT, 128), jnp.float32)
            back[q, t] = jnp.zeros((EXT, 128), jnp.float32)

    def fill_own(n, carry):
        angle = half * COLUMN + order[n]
        tap_tables(mag_ref[angle], offset_ref[angle].astype(jnp.float32), index_ref, weight_ref, 2 * n)
        return carry

    lax.fori_loop(0, COLUMN, fill_own, 0)

    def near_values():
        pair_values.wait_recv()
        local = pltpu.make_async_copy(pair_vmem, pair_ref, local_sem.at[1])
        local.start()
        for p in (1, 2):
            values_on(p)
        values_copy(0, OTHER[0], "core").wait_recv()
        near = to_smem(1, 5, 2)
        near.start()
        near.wait()
        local.wait()

    def core_values():
        for p in range(1, 5):
            values_copy(0, OTHER[p], "core").wait_recv()
        core = to_smem(OTHER[1], 4, 2)
        core.start()
        core.wait()

    def far_values():
        for p in (5, 6, 7):
            values_on(p)

    def last_values():
        for p in (5, 6, 7):
            values_copy(0, OTHER[p], "core").wait_recv()
        far = to_smem(OWN[5], 6, 2)
        far.start()
        far.wait()

    def fill_pair():
        def one(n, carry):
            angle = half * COLUMN + order[n]
            tap_tables(pair_ref[0, angle], pair_ref[1, angle], index_ref, weight_ref, 2 * n + 1)
            return carry

        lax.fori_loop(0, COLUMN, one, 0)

    images = (image_0, image_1)
    exchanged = []

    def start(copy):
        copy.start()
        exchanged.append(copy)

    def tiles_apart(ref, tile, phase, after):
        def finish(slot):
            for q in (1, 0):
                values = tile(slot, q)
                for t in range(TILES):
                    store_total(ref, q, t, values(t, load_total(ref, q, t)))
                    if q:
                        start(pair_copy(ref.at[1, t], other.at[phase, t], 2 + TILES * phase + t))
                of, n = (pair, 4 * phase + 2) if q else (band, 4 * phase)
                start(slab_copy(ref.at[q, :, pl.ds(ROWS, 8)], below.at[phase, q], n, 1, of))
                start(slab_copy(ref.at[q, :, pl.ds(0, 8)], above.at[phase, q], n + 1, SLABS - 1, of))
                after(q)

        return finish

    def each(ref, tile):
        def compute(slot):
            for q in range(2):
                values = tile(slot, q)
                for t in range(TILES):
                    store_total(ref, q, t, values(t, load_total(ref, q, t)))

        return compute

    def full_rows(ref, t, phase):
        for g in range(EXT // 8):
            value = ref[0, t, 8 * g : 8 * g + 8, :] + other[phase, t, 8 * g : 8 * g + 8, :]
            if g == 0:
                value = value + jnp.where(slab > 0, below[phase, 0, t] + below[phase, 1, t], 0.0)
            if g == EXT // 8 - 1:
                value = value + jnp.where(slab < SLABS - 1, above[phase, 0, t] + above[phase, 1, t], 0.0)
            ext[t, 8 * g : 8 * g + 8, :] = value

    def project(slot, q):
        angle = pair if q else band
        mag, offset, shift = (tables[slot, n, angle] for n in range(3))
        shift = jnp.clip(shift.astype(jnp.int32), -HALO, HALO)
        return lambda t, total: project_tile(vols, slot, t, mag, offset, shift, images[q], total)

    def send_sums(q):
        for t in range(TILES):
            column = jnp.zeros((1, 128), jnp.float32)
            for g in range(EXT // 8):
                value = proj[q, t, 8 * g : 8 * g + 8, :]
                if g == 0:
                    value = jnp.where(row + slab * ROWS >= HALO, value, 0.0)
                if g == EXT // 8 - 1:
                    value = jnp.where((row < HALO) | (slab < SLABS - 1), value, 0.0)
                column = column + jnp.sum(value, axis=0, keepdims=True)
            own_sums[q, t : t + 1, :] = column
        if q:
            start(pair_copy(own_sums.at[1], sums.at[SLABS], 1))
        for j in range(1, SLABS):
            start(slab_copy(own_sums.at[q], sums.at[SLABS * q + j], 7 + 7 * q + j, j, pair if q else band))

    own_seen.wait()
    for t in range(TILES):
        column = jnp.sum(seen[:, 128 * t : 128 * t + 128], axis=0, keepdims=True)
        own_sums[0, TILES + t : TILES + t + 1, :] = column
        own_sums[1, TILES + t : TILES + t + 1, :] = jnp.zeros((1, 128), jnp.float32)
    own_block.wait()
    own_table.wait()
    hooks = {
        "first": lambda: [hear(0), tell(1)],
        "far": lambda: [values_on(3), values_on(4)],
        1: near_values,
        6: core_values,
        7: lambda: hear(1),
        8: far_values,
        9: last_values,
    }
    gather.run(each(proj, project), tiles_apart(proj, project, 0, send_sums), hooks)
    fill_pair()
    for copy in exchanged:
        copy.wait_recv()

    all_sums = own_sums[0]
    for j in range(1, 2 * SLABS):
        all_sums = all_sums + sums[j]
    for t in range(TILES):
        full_rows(proj, t, 0)
        gain = all_sums[TILES + t : TILES + t + 1, :] / all_sums[t : t + 1, :]
        gain = jnp.broadcast_to(gain, (8, 128))
        for g in range(ROWS // 8):
            value = seen[8 * g : 8 * g + 8, 128 * t : 128 * t + 128]
            value = value - gain * ext[t, HALO + 8 * g : HALO + 8 * g + 8, :]
            residual_ref[0, 8 * g : 8 * g + 8, 128 * t : 128 * t + 128] = value
    double = 2 * (lane & 63)
    for k in range(2):
        for phase in range(2):
            for g in range(ROWS // 8):
                a = residual_ref[0, 8 * g : 8 * g + 8, 256 * k : 256 * k + 128]
                b = residual_ref[0, 8 * g : 8 * g + 8, 256 * k + 128 : 256 * k + 256]
                first = ROWS * (2 * k + phase) + 8 * g
                value = jnp.where(lane < 64, take(a, double + phase), take(b, double + phase))
                ress[0, first : first + 8, :] = value

    spread_out = Gather(ress, RES_PARTS, res_send, res_recv, place)
    spread_out.start()

    def backproject(slot, q):
        angle = half * COLUMN + order[slot]
        shift = pair_ref[2, angle].astype(jnp.int32) if q else shift_ref[angle]
        shift = jnp.clip(shift, -HALO, HALO)
        return lambda t, total: backproject_tile(
            ress, slot, t, 2 * slot + q, shift, index_ref, weight_ref, images[q], total
        )

    before = len(exchanged)
    spread_out.run(each(back, backproject), tiles_apart(back, backproject, 1, lambda q: None))
    for copy in exchanged[before:]:
        copy.wait_recv()
    for t in range(TILES):
        full_rows(back, t, 1)
        correction_ref[0, :, 128 * t : 128 * (t + 1)] = ext[t, HALO : HALO + ROWS, :]
    gather.finish()
    spread_out.finish()
    for route in routes:
        values_copy(*route).wait_send()
    for copy in [pair_values, *exchanged]:
        copy.wait_send()


def shards(volume, measured, magnification, shift_y, shift_z):
    hbm, vmem = pl.BlockSpec(memory_space=pltpu.HBM), pl.BlockSpec(memory_space=pltpu.VMEM)
    block = jax.ShapeDtypeStruct(volume.shape, jnp.float32)
    f32 = jnp.float32
    arguments = (*(x.reshape(BANDS) for x in (magnification, shift_y, shift_z)), volume, measured)
    residual, correction = pl.pallas_call(
        kernel,
        out_shape=(block, block),
        in_specs=[hbm] * 5,
        out_specs=(vmem, vmem),
        scratch_shapes=[
            pltpu.SMEM((BANDS,), f32),
            pltpu.SMEM((BANDS,), jnp.int32),
            pltpu.SMEM((BANDS,), jnp.int32),
            pltpu.SMEM((COLUMN,), jnp.int32),
            pltpu.VMEM((COLUMN, ROWS, 128 * TILES), f32),
            pltpu.VMEM((COLUMN, RES_ROWS, 128), f32),
            pltpu.VMEM((COLUMN, 8, 128), f32),
            pltpu.SMEM((COLUMN, 8, 128), f32),
            pltpu.VMEM((8, 128), f32),
            pltpu.SMEM((8, 128), f32),
            pltpu.VMEM((ROWS, 128 * TILES), f32),
            pltpu.VMEM((2, TILES, EXT, 128), f32),
            pltpu.VMEM((2, TILES, EXT, 128), f32),
            pltpu.VMEM((2, TILES, EXT, 128), f32),
            pltpu.VMEM((TILES, EXT, 128), f32),
            pltpu.VMEM((2, 8, 128), f32),
            pltpu.VMEM((2 * SLABS, 8, 128), f32),
            pltpu.VMEM((2, 2, TILES, 8, 128), f32),
            pltpu.VMEM((2, 2, TILES, 8, 128), f32),
            pltpu.VMEM((BANDS, 128, 128), jnp.int32),
            pltpu.VMEM((BANDS, 128, 128), f32),
            pltpu.VMEM((TILES, ROWS + 16, 128), f32),
            pltpu.VMEM((TILES, ROWS + 16, 128), f32),
            pltpu.SemaphoreType.DMA((COPIES,)),
            pltpu.SemaphoreType.DMA((COPIES,)),
            pltpu.SemaphoreType.DMA((COPIES,)),
            pltpu.SemaphoreType.DMA((COPIES,)),
            pltpu.SemaphoreType.DMA((22,)),
            pltpu.SemaphoreType.DMA((22,)),
            pltpu.SemaphoreType.DMA((2 + 2 * TILES,)),
            pltpu.SemaphoreType.DMA((2 + 2 * TILES,)),
            pltpu.SemaphoreType.DMA((COLUMN,)),
            pltpu.SemaphoreType.DMA((COLUMN,)),
            pltpu.SemaphoreType.DMA((5,)),
            pltpu.SemaphoreType.REGULAR((2, 2)),
        ],
        compiler_params=pltpu.CompilerParams(
            collective_id=0, has_side_effects=True, vmem_limit_bytes=40 * 1024 * 1024
        ),
        name="sirt",
    )(*(pltpu.with_memory_space_constraint(x, pltpu.HBM) for x in arguments))
    return residual * (1.0 / BANDS), correction * (1.0 / (BANDS * math.sqrt(BANDS)))


def solution(mesh):
    return jax.shard_map(
        shards,
        mesh=mesh,
        in_specs=(
            P("xband", "zslab", None),
            P("xband", "zslab", None),
            P(None, "xband"),
            P(None, "xband"),
            P(None, "xband"),
        ),
        out_specs=(P("xband", "zslab", None), P("xband", "zslab", None)),
        check_vma=False,
    )
```

```python
import functools
import math

import jax
import jax.numpy as jnp
from jax import lax
from jax.experimental import pallas as pl
from jax.experimental.pallas import tpu as pltpu
from jax.sharding import PartitionSpec as P

HALO = 4
TILES = 4
ROWS = 32
EXT = ROWS + 2 * HALO
SLABS = 8
RING = 8
BANDS = 32
CENTRE = 255.5
RES_ROWS = TILES * ROWS
VOL_PARTS = ((0, 16), (16, 16), (0, 32))
RES_PARTS = ((0, 64), (64, 64), (0, 128))
COPIES = 20
COLUMN = 16
FORWARD_TILES = ((0, 1), (0, 1, 2), (1, 2, 3), (2, 3))
BACKWARD_TILES = ((0,), (0, 1), (0, 1), (1,))
MESH = pl.DeviceIdType.MESH


def take(x, index):
    return jnp.take_along_axis(x, index, axis=1, mode="promise_in_bounds")


def iota(axis):
    return lax.broadcasted_iota(jnp.int32, (8, 128), axis)


def take_tiles(tiles, index):
    lanes = index & 127
    values = None
    for k, groups in tiles.items():
        part = [take(x, lanes) for x in groups]
        if values is None:
            values = part
        else:
            here = index >= 128 * k
            values = [jnp.where(here, p, v) for p, v in zip(part, values)]
    return values


def moved(work, tile, shift, total):
    return [t + work[tile, pl.ds(8 + 8 * g - HALO - shift, 8), :] for g, t in enumerate(total)]


def project_tile(blocks, slot, ub, mag, offset, shift, work, total):
    mag = jnp.full((8, 128), mag, jnp.float32)
    u = (iota(1) + 128 * ub).astype(jnp.float32)
    target = (u - CENTRE) / mag + CENTRE + offset
    lower = jnp.floor(target)
    frac = target - lower
    left = lower.astype(jnp.int32)
    tiles = {
        k: [blocks[slot, 8 * g : 8 * g + 8, 128 * k : 128 * k + 128] for g in range(ROWS // 8)]
        for k in FORWARD_TILES[ub]
    }
    a = take_tiles(tiles, left)
    b = take_tiles(tiles, left + 1)
    for g in range(ROWS // 8):
        work[ub, 8 + 8 * g : 16 + 8 * g, :] = (1.0 - frac) * a[g] + frac * b[g]
    return moved(work, ub, shift, total)


def tap_tables(mag, offset, index_ref, weight_ref, angle):
    lane = iota(1)
    mag = jnp.full((8, 128), mag, jnp.float32)
    for yb in range(TILES):
        y = (lane + 128 * yb).astype(jnp.float32)
        middle = (y - CENTRE - offset) * mag + CENTRE
        for phase in range(2):
            first = jnp.floor((middle - phase) * 0.5).astype(jnp.int32)
            for tap in range(2):
                j = first + tap
                u = (2 * j + phase).astype(jnp.float32)
                target = (u - CENTRE) / mag + CENTRE + offset
                weight = jnp.maximum(0.0, 1.0 - jnp.abs(y - target))
                weight = jnp.where((j >= 0) & (j < 256), weight, 0.0)
                n = 8 * (yb * 4 + phase * 2 + tap)
                index_ref[angle, n : n + 8, :] = jnp.clip(j, 0, 255)
                weight_ref[angle, n : n + 8, :] = weight


def backproject_tile(blocks, slot, yb, angle, shift, index_ref, weight_ref, work, total):
    image = [jnp.zeros((8, 128), jnp.float32)] * (ROWS // 8)
    for phase in range(2):
        tiles = {}
        for k in BACKWARD_TILES[yb]:
            start = ROWS * (2 * k + phase)
            tiles[k] = [blocks[slot, start + 8 * g : start + 8 * g + 8, :] for g in range(ROWS // 8)]
        for tap in range(2):
            n = 8 * (4 * yb + 2 * phase + tap)
            values = take_tiles(tiles, index_ref[angle, n : n + 8, :])
            weight = weight_ref[angle, n : n + 8, :]
            image = [i + weight * v for i, v in zip(image, values)]
    for g, value in enumerate(image):
        work[yb, 8 + 8 * g : 16 + 8 * g, :] = value
    return moved(work, yb, -shift, total)


OWN = (0, 2, 3, 4, 5, 10, 11, 12)
OTHER = (1, 6, 7, 8, 9, 13, 14, 15)
AWAY = (0, 1, -1, 2, -2, 3, -3, 4)


class Gather:
    def __init__(self, blocks, parts, send, recv, place, own=None):
        self.blocks, self.parts, self.send_sem, self.recv_sem = blocks, parts, send, recv
        self.place = place
        self.own = blocks.at[0] if own is None else own
        self.sent = []

    def copy(self, source, target, part, n, to):
        rows = pl.ds(*self.parts[part])
        return pltpu.make_async_remote_copy(
            src_ref=source.at[rows],
            dst_ref=self.blocks.at[target, rows],
            send_sem=self.send_sem.at[n],
            recv_sem=self.recv_sem.at[n],
            device_id={"xband": self.place[to]},
            device_id_type=MESH,
        )

    def send(self, source, target, part, n, to):
        self.copy(self.blocks.at[source] if source else self.own, target, part, n, to).start()
        self.sent.append((source, target, part, n, to))

    def wait(self, slot, part, n):
        self.copy(self.blocks.at[slot], slot, part, n, "core").wait_recv()

    def start(self):
        for part in range(2):
            self.send(0, OWN[3], part, 2 + part, "long2")
            self.send(0, OWN[4], part, 4 + part, "short2")
        self.send(0, OWN[1], 2, 0, "long1")
        self.send(0, OWN[2], 2, 1, "short1")
        self.core(0)

    def core(self, p):
        self.send(OWN[p], OTHER[p], 2, 12 + p, "core")

    def from_core(self, p):
        self.wait(OTHER[p], 2, 12 + p)

    def run(self, compute, finish, hooks=None):
        hooks = hooks or {}
        def first():
            if "first" in hooks:
                hooks["first"]()
            for part in range(2):
                self.wait(OWN[3], part, 2 + part)
                self.send(OWN[3], OWN[5], part, 6 + part, "long1")
                self.send(OWN[3], OWN[7], part, 8 + part, "long2")
                self.wait(OWN[4], part, 4 + part)
                self.send(OWN[4], OWN[6], part, 10 + part, "short1")
                if "far" in hooks and part == 0:
                    hooks["far"]()
            self.core(3)
            self.core(4)
            for n, p in enumerate((1, 2)):
                self.wait(OWN[p], 2, n)
                self.core(p)
            self.from_core(0)

        def last():
            for p, n in ((5, 6), (6, 10), (7, 8)):
                self.wait(OWN[p], 0, n)
                self.wait(OWN[p], 1, n + 1)
                self.core(p)

        actions = {1: first, OWN[5]: last}
        for p in range(1, RING - 1):
            actions[OTHER[p]] = functools.partial(self.from_core, p)

        def one(slot, carry):
            for n, action in actions.items():
                pl.when(slot == n)(action)
                if n in hooks:
                    pl.when(slot == n)(hooks[n])
            compute(slot)
            return carry

        lax.fori_loop(0, COLUMN - 1, one, 0)
        self.from_core(RING - 1)
        finish(COLUMN - 1)

    def finish(self):
        for source, *rest in self.sent:
            self.copy(self.blocks.at[source] if source else self.own, *rest).wait_send()


def load_total(ref, q, t):
    return [ref[q, t, 8 * g : 8 * g + 8, :] for g in range(EXT // 8)]


def store_total(ref, q, t, total):
    for g, value in enumerate(total):
        ref[q, t, 8 * g : 8 * g + 8, :] = value


def kernel(
    mag_hbm, offset_hbm, shift_hbm, volume_ref, measured_ref, residual_ref, correction_ref,
    mag_ref, offset_ref, shift_ref, order,
    vols, ress, tables_vmem, tables, pair_vmem, pair_ref, seen, proj, back, other, ext, own_sums, sums,
    below, above, index_ref, weight_ref, image_0, image_1,
    vol_send, vol_recv, res_send, res_recv, slab_send, slab_recv, pair_send, pair_recv,
    values_send, values_recv, local_sem, word_sem,
):
    slab, band = lax.axis_index("zslab"), lax.axis_index("xband")
    half, core = lax.div(band, 16), lax.rem(band, 2)
    z = lax.div(lax.rem(band, 16), 2)
    turn = 1 - 2 * core
    pair = (1 - half) * COLUMN + lax.rem(band, COLUMN)

    def ring(away, core=core):
        return half * COLUMN + lax.rem(z + away + 2 * RING, RING) * 2 + core

    scalars = [
        pltpu.make_async_copy(source, target, local_sem.at[n])
        for n, (source, target) in enumerate(
            ((mag_hbm, mag_ref), (offset_hbm, offset_ref), (shift_hbm, shift_ref))
        )
    ]
    own_block = pltpu.make_async_copy(volume_ref.at[0], vols.at[0], local_sem.at[3])
    own_seen = pltpu.make_async_copy(measured_ref.at[0], seen, local_sem.at[4])
    for copy in [*scalars, own_block, own_seen]:
        copy.start()

    place = {
        "long1": ring(turn),
        "long2": ring(2 * turn),
        "short1": ring(-turn),
        "short2": ring(-2 * turn),
        "core": band + turn,
        "pair": pair,
    }
    for p, away in enumerate(AWAY):
        order[OWN[p]] = lax.rem(z - turn * away + 2 * RING, RING) * 2 + core
        order[OTHER[p]] = lax.rem(z + turn * away + 2 * RING, RING) * 2 + 1 - core
    barrier = pltpu.get_barrier_semaphore()
    for to in place.values():
        pl.semaphore_signal(barrier, inc=1, device_id={"xband": to}, device_id_type=MESH)
    slabs = [lax.rem(slab + j, SLABS) for j in range(SLABS)]
    for to in (slabs[1], slabs[SLABS - 1]):
        for of in (band, pair):
            pl.semaphore_signal(barrier, inc=1, device_id={"zslab": to, "xband": of}, device_id_type=MESH)

    pl.semaphore_wait(barrier, len(place) + 4)

    gather = Gather(vols, VOL_PARTS, vol_send, vol_recv, place, volume_ref.at[0])
    gather.start()

    lane, row = iota(1), iota(0)
    for copy in scalars:
        copy.wait()

    def spread(angle, values):
        here = lane == angle
        mags, offsets, shifts = values
        return (
            jnp.where(here, mag_ref[angle], mags),
            jnp.where(here, offset_ref[angle].astype(jnp.float32), offsets),
            jnp.where(here, shift_ref[angle].astype(jnp.float32), shifts),
        )

    zeros = jnp.zeros((8, 128), jnp.float32)
    mags, offsets, shifts = lax.fori_loop(0, BANDS, spread, (zeros, zeros, zeros))
    tables_vmem[0] = jnp.where(row == 0, mags, jnp.where(row == 1, offsets, shifts))

    def tell(n):
        for side, to in enumerate((slabs[n + 1], slabs[SLABS - 1 - n])):
            pl.semaphore_signal(word_sem.at[n, side], inc=1, device_id={"zslab": to}, device_id_type=MESH)

    def hear(n):
        for side in range(2):
            pl.semaphore_wait(word_sem.at[n, side], 1)

    tell(0)

    def pair_copy(source, target, n):
        return pltpu.make_async_remote_copy(
            src_ref=source,
            dst_ref=target,
            send_sem=pair_send.at[n],
            recv_sem=pair_recv.at[n],
            device_id={"xband": pair},
            device_id_type=MESH,
        )

    def slab_copy(source, target, n, to, of=band):
        return pltpu.make_async_remote_copy(
            src_ref=source,
            dst_ref=target,
            send_sem=slab_send.at[n],
            recv_sem=slab_recv.at[n],
            device_id={"zslab": slabs[to], "xband": of},
            device_id_type=MESH,
        )

    pair_values = pair_copy(tables_vmem.at[0], pair_vmem, 0)
    pair_values.start()
    def values_copy(source, target, to):
        return pltpu.make_async_remote_copy(
            src_ref=tables_vmem.at[source],
            dst_ref=tables_vmem.at[target],
            send_sem=values_send.at[target],
            recv_sem=values_recv.at[target],
            device_id={"xband": place[to]},
            device_id_type=MESH,
        )

    routes = (
        (0, OWN[3], "long2"), (0, OWN[4], "short2"), (0, OWN[1], "long1"), (0, OWN[2], "short1"),
        (OWN[3], OWN[7], "long2"), (OWN[3], OWN[5], "long1"), (OWN[4], OWN[6], "short1"),
        *((OWN[p], OTHER[p], "core") for p in range(RING)),
    )
    for route in (*routes[:4], routes[7]):
        values_copy(*route).start()

    def values_on(p):
        values_copy(0, OWN[p], "core").wait_recv()
        for route in routes:
            if route[0] == OWN[p]:
                values_copy(*route).start()

    def to_smem(first, count, n):
        rows = pl.ds(first, count)
        return pltpu.make_async_copy(tables_vmem.at[rows], tables.at[rows], local_sem.at[n])

    own_table = pltpu.make_async_copy(tables_vmem.at[0], tables.at[0], local_sem.at[0])
    own_table.start()
    for t in range(TILES):
        for image in (image_0, image_1):
            image[t, 0:8, :] = zeros
            image[t, 8 + ROWS :, :] = zeros
        for q in range(2):
            proj[q, t] = jnp.zeros((EXT, 128), jnp.float32)
            back[q, t] = jnp.zeros((EXT, 128), jnp.float32)

    def fill_own(n, carry):
        angle = half * COLUMN + order[n]
        tap_tables(mag_ref[angle], offset_ref[angle].astype(jnp.float32), index_ref, weight_ref, 2 * n)
        return carry

    lax.fori_loop(0, COLUMN, fill_own, 0)

    def near_values():
        pair_values.wait_recv()
        local = pltpu.make_async_copy(pair_vmem, pair_ref, local_sem.at[1])
        local.start()
        for p in (1, 2):
            values_on(p)
        values_copy(0, OTHER[0], "core").wait_recv()
        near = to_smem(1, 5, 2)
        near.start()
        near.wait()
        local.wait()

    def core_values():
        for p in range(1, 5):
            values_copy(0, OTHER[p], "core").wait_recv()
        core = to_smem(OTHER[1], 4, 2)
        core.start()
        core.wait()

    def far_values():
        for p in (5, 6, 7):
            values_on(p)

    def last_values():
        for p in (5, 6, 7):
            values_copy(0, OTHER[p], "core").wait_recv()
        far = to_smem(OWN[5], 6, 2)
        far.start()
        far.wait()

    def fill_pair():
        def one(n, carry):
            angle = half * COLUMN + order[n]
            tap_tables(pair_ref[0, angle], pair_ref[1, angle], index_ref, weight_ref, 2 * n + 1)
            return carry

        lax.fori_loop(0, COLUMN, one, 0)

    images = (image_0, image_1)
    exchanged = []

    def start(copy):
        copy.start()
        exchanged.append(copy)

    def tiles_apart(ref, tile, phase, after):
        def finish(slot):
            for q in (1, 0):
                values = tile(slot, q)
                for t in range(TILES):
                    store_total(ref, q, t, values(t, load_total(ref, q, t)))
                    if q:
                        start(pair_copy(ref.at[1, t], other.at[phase, t], 2 + TILES * phase + t))
                of, n = (pair, 4 * phase + 2) if q else (band, 4 * phase)
                start(slab_copy(ref.at[q, :, pl.ds(ROWS, 8)], below.at[phase, q], n, 1, of))
                start(slab_copy(ref.at[q, :, pl.ds(0, 8)], above.at[phase, q], n + 1, SLABS - 1, of))
                after(q)

        return finish

    def each(ref, tile):
        def compute(slot):
            for q in range(2):
                values = tile(slot, q)
                for t in range(TILES):
                    store_total(ref, q, t, values(t, load_total(ref, q, t)))

        return compute

    def full_rows(ref, t, phase):
        for g in range(EXT // 8):
            value = ref[0, t, 8 * g : 8 * g + 8, :] + other[phase, t, 8 * g : 8 * g + 8, :]
            if g == 0:
                value = value + jnp.where(slab > 0, below[phase, 0, t] + below[phase, 1, t], 0.0)
            if g == EXT // 8 - 1:
                value = value + jnp.where(slab < SLABS - 1, above[phase, 0, t] + above[phase, 1, t], 0.0)
            ext[t, 8 * g : 8 * g + 8, :] = value

    def project(slot, q):
        angle = pair if q else band
        mag, offset, shift = (tables[slot, n, angle] for n in range(3))
        shift = jnp.clip(shift.astype(jnp.int32), -HALO, HALO)
        return lambda t, total: project_tile(vols, slot, t, mag, offset, shift, images[q], total)

    def send_sums(q):
        for t in range(TILES):
            column = jnp.zeros((1, 128), jnp.float32)
            for g in range(EXT // 8):
                value = proj[q, t, 8 * g : 8 * g + 8, :]
                if g == 0:
                    value = jnp.where(row + slab * ROWS >= HALO, value, 0.0)
                if g == EXT // 8 - 1:
                    value = jnp.where((row < HALO) | (slab < SLABS - 1), value, 0.0)
                column = column + jnp.sum(value, axis=0, keepdims=True)
            own_sums[q, t : t + 1, :] = column
        if q:
            start(pair_copy(own_sums.at[1], sums.at[SLABS], 1))
        for j in range(1, SLABS):
            start(slab_copy(own_sums.at[q], sums.at[SLABS * q + j], 7 + 7 * q + j, j, pair if q else band))

    own_seen.wait()
    for t in range(TILES):
        column = jnp.sum(seen[:, 128 * t : 128 * t + 128], axis=0, keepdims=True)
        own_sums[0, TILES + t : TILES + t + 1, :] = column
        own_sums[1, TILES + t : TILES + t + 1, :] = jnp.zeros((1, 128), jnp.float32)
    own_block.wait()
    own_table.wait()
    hooks = {
        "first": lambda: [hear(0), tell(1)],
        "far": lambda: [values_on(3), values_on(4)],
        1: near_values,
        6: core_values,
        14: lambda: hear(1),
        9: far_values,
        10: last_values,
    }
    gather.run(each(proj, project), tiles_apart(proj, project, 0, send_sums), hooks)
    fill_pair()
    for copy in exchanged:
        copy.wait_recv()

    all_sums = own_sums[0]
    for j in range(1, 2 * SLABS):
        all_sums = all_sums + sums[j]
    for t in range(TILES):
        full_rows(proj, t, 0)
        gain = all_sums[TILES + t : TILES + t + 1, :] / all_sums[t : t + 1, :]
        gain = jnp.broadcast_to(gain, (8, 128))
        for g in range(ROWS // 8):
            value = seen[8 * g : 8 * g + 8, 128 * t : 128 * t + 128]
            value = value - gain * ext[t, HALO + 8 * g : HALO + 8 * g + 8, :]
            residual_ref[0, 8 * g : 8 * g + 8, 128 * t : 128 * t + 128] = value
    double = 2 * (lane & 63)
    for k in range(2):
        for phase in range(2):
            for g in range(ROWS // 8):
                a = residual_ref[0, 8 * g : 8 * g + 8, 256 * k : 256 * k + 128]
                b = residual_ref[0, 8 * g : 8 * g + 8, 256 * k + 128 : 256 * k + 256]
                first = ROWS * (2 * k + phase) + 8 * g
                value = jnp.where(lane < 64, take(a, double + phase), take(b, double + phase))
                ress[0, first : first + 8, :] = value

    spread_out = Gather(ress, RES_PARTS, res_send, res_recv, place)
    spread_out.start()

    def backproject(slot, q):
        angle = half * COLUMN + order[slot]
        shift = pair_ref[2, angle].astype(jnp.int32) if q else shift_ref[angle]
        shift = jnp.clip(shift, -HALO, HALO)
        return lambda t, total: backproject_tile(
            ress, slot, t, 2 * slot + q, shift, index_ref, weight_ref, images[q], total
        )

    before = len(exchanged)
    spread_out.run(each(back, backproject), tiles_apart(back, backproject, 1, lambda q: None))
    for copy in exchanged[before:]:
        copy.wait_recv()
    for t in range(TILES):
        full_rows(back, t, 1)
        correction_ref[0, :, 128 * t : 128 * (t + 1)] = ext[t, HALO : HALO + ROWS, :]
    gather.finish()
    spread_out.finish()
    for route in routes:
        values_copy(*route).wait_send()
    for copy in [pair_values, *exchanged]:
        copy.wait_send()


def shards(volume, measured, magnification, shift_y, shift_z):
    hbm, vmem = pl.BlockSpec(memory_space=pltpu.HBM), pl.BlockSpec(memory_space=pltpu.VMEM)
    block = jax.ShapeDtypeStruct(volume.shape, jnp.float32)
    f32 = jnp.float32
    arguments = (*(x.reshape(BANDS) for x in (magnification, shift_y, shift_z)), volume, measured)
    residual, correction = pl.pallas_call(
        kernel,
        out_shape=(block, block),
        in_specs=[hbm] * 5,
        out_specs=(vmem, vmem),
        scratch_shapes=[
            pltpu.SMEM((BANDS,), f32),
            pltpu.SMEM((BANDS,), jnp.int32),
            pltpu.SMEM((BANDS,), jnp.int32),
            pltpu.SMEM((COLUMN,), jnp.int32),
            pltpu.VMEM((COLUMN, ROWS, 128 * TILES), f32),
            pltpu.VMEM((COLUMN, RES_ROWS, 128), f32),
            pltpu.VMEM((COLUMN, 8, 128), f32),
            pltpu.SMEM((COLUMN, 8, 128), f32),
            pltpu.VMEM((8, 128), f32),
            pltpu.SMEM((8, 128), f32),
            pltpu.VMEM((ROWS, 128 * TILES), f32),
            pltpu.VMEM((2, TILES, EXT, 128), f32),
            pltpu.VMEM((2, TILES, EXT, 128), f32),
            pltpu.VMEM((2, TILES, EXT, 128), f32),
            pltpu.VMEM((TILES, EXT, 128), f32),
            pltpu.VMEM((2, 8, 128), f32),
            pltpu.VMEM((2 * SLABS, 8, 128), f32),
            pltpu.VMEM((2, 2, TILES, 8, 128), f32),
            pltpu.VMEM((2, 2, TILES, 8, 128), f32),
            pltpu.VMEM((BANDS, 128, 128), jnp.int32),
            pltpu.VMEM((BANDS, 128, 128), f32),
            pltpu.VMEM((TILES, ROWS + 16, 128), f32),
            pltpu.VMEM((TILES, ROWS + 16, 128), f32),
            pltpu.SemaphoreType.DMA((COPIES,)),
            pltpu.SemaphoreType.DMA((COPIES,)),
            pltpu.SemaphoreType.DMA((COPIES,)),
            pltpu.SemaphoreType.DMA((COPIES,)),
            pltpu.SemaphoreType.DMA((22,)),
            pltpu.SemaphoreType.DMA((22,)),
            pltpu.SemaphoreType.DMA((2 + 2 * TILES,)),
            pltpu.SemaphoreType.DMA((2 + 2 * TILES,)),
            pltpu.SemaphoreType.DMA((COLUMN,)),
            pltpu.SemaphoreType.DMA((COLUMN,)),
            pltpu.SemaphoreType.DMA((5,)),
            pltpu.SemaphoreType.REGULAR((2, 2)),
        ],
        compiler_params=pltpu.CompilerParams(
            collective_id=0, has_side_effects=True, vmem_limit_bytes=40 * 1024 * 1024
        ),
        name="sirt",
    )(*(pltpu.with_memory_space_constraint(x, pltpu.HBM) for x in arguments))
    return residual * (1.0 / BANDS), correction * (1.0 / (BANDS * math.sqrt(BANDS)))


def solution(mesh):
    return jax.shard_map(
        shards,
        mesh=mesh,
        in_specs=(
            P("xband", "zslab", None),
            P("xband", "zslab", None),
            P(None, "xband"),
            P(None, "xband"),
            P(None, "xband"),
        ),
        out_specs=(P("xband", "zslab", None), P("xband", "zslab", None)),
        check_vma=False,
    )
```

```python
import functools
import math

import jax
import jax.numpy as jnp
from jax import lax
from jax.experimental import pallas as pl
from jax.experimental.pallas import tpu as pltpu
from jax.sharding import PartitionSpec as P

HALO = 4
TILES = 4
ROWS = 32
EXT = ROWS + 2 * HALO
SLABS = 8
RING = 8
BANDS = 32
CENTRE = 255.5
RES_ROWS = TILES * ROWS
VOL_PARTS = ((0, 16), (16, 16), (0, 32))
RES_PARTS = ((0, 64), (64, 64), (0, 128))
COPIES = 20
COLUMN = 16
FORWARD_TILES = ((0, 1), (0, 1, 2), (1, 2, 3), (2, 3))
BACKWARD_TILES = ((0,), (0, 1), (0, 1), (1,))
MESH = pl.DeviceIdType.MESH


def take(x, index):
    return jnp.take_along_axis(x, index, axis=1, mode="promise_in_bounds")


def iota(axis):
    return lax.broadcasted_iota(jnp.int32, (8, 128), axis)


def take_tiles(tiles, index):
    lanes = index & 127
    values = None
    for k, groups in tiles.items():
        part = [take(x, lanes) for x in groups]
        if values is None:
            values = part
        else:
            here = index >= 128 * k
            values = [jnp.where(here, p, v) for p, v in zip(part, values)]
    return values


def moved(work, tile, shift, total):
    return [t + work[tile, pl.ds(8 + 8 * g - HALO - shift, 8), :] for g, t in enumerate(total)]


def project_tile(blocks, slot, ub, mag, offset, shift, work, total):
    mag = jnp.full((8, 128), mag, jnp.float32)
    u = (iota(1) + 128 * ub).astype(jnp.float32)
    target = (u - CENTRE) / mag + CENTRE + offset
    lower = jnp.floor(target)
    frac = target - lower
    left = lower.astype(jnp.int32)
    tiles = {
        k: [blocks[slot, 8 * g : 8 * g + 8, 128 * k : 128 * k + 128] for g in range(ROWS // 8)]
        for k in FORWARD_TILES[ub]
    }
    a = take_tiles(tiles, left)
    b = take_tiles(tiles, left + 1)
    for g in range(ROWS // 8):
        work[ub, 8 + 8 * g : 16 + 8 * g, :] = (1.0 - frac) * a[g] + frac * b[g]
    return moved(work, ub, shift, total)


def tap_tables(mag, offset, index_ref, weight_ref, angle):
    lane = iota(1)
    mag = jnp.full((8, 128), mag, jnp.float32)
    for yb in range(TILES):
        y = (lane + 128 * yb).astype(jnp.float32)
        middle = (y - CENTRE - offset) * mag + CENTRE
        for phase in range(2):
            first = jnp.floor((middle - phase) * 0.5).astype(jnp.int32)
            for tap in range(2):
                j = first + tap
                u = (2 * j + phase).astype(jnp.float32)
                target = (u - CENTRE) / mag + CENTRE + offset
                weight = jnp.maximum(0.0, 1.0 - jnp.abs(y - target))
                weight = jnp.where((j >= 0) & (j < 256), weight, 0.0)
                n = 8 * (yb * 4 + phase * 2 + tap)
                index_ref[angle, n : n + 8, :] = jnp.clip(j, 0, 255)
                weight_ref[angle, n : n + 8, :] = weight


def backproject_tile(blocks, slot, yb, angle, shift, index_ref, weight_ref, work, total):
    image = [jnp.zeros((8, 128), jnp.float32)] * (ROWS // 8)
    for phase in range(2):
        tiles = {}
        for k in BACKWARD_TILES[yb]:
            start = ROWS * (2 * k + phase)
            tiles[k] = [blocks[slot, start + 8 * g : start + 8 * g + 8, :] for g in range(ROWS // 8)]
        for tap in range(2):
            n = 8 * (4 * yb + 2 * phase + tap)
            values = take_tiles(tiles, index_ref[angle, n : n + 8, :])
            weight = weight_ref[angle, n : n + 8, :]
            image = [i + weight * v for i, v in zip(image, values)]
    for g, value in enumerate(image):
        work[yb, 8 + 8 * g : 16 + 8 * g, :] = value
    return moved(work, yb, -shift, total)


OWN = (0, 2, 3, 4, 5, 10, 11, 12)
OTHER = (1, 6, 7, 8, 9, 13, 14, 15)
AWAY = (0, 1, -1, 2, -2, 3, -3, 4)


class Gather:
    def __init__(self, blocks, parts, send, recv, place, own=None):
        self.blocks, self.parts, self.send_sem, self.recv_sem = blocks, parts, send, recv
        self.place = place
        self.own = blocks.at[0] if own is None else own
        self.sent = []

    def copy(self, source, target, part, n, to):
        rows = pl.ds(*self.parts[part])
        return pltpu.make_async_remote_copy(
            src_ref=source.at[rows],
            dst_ref=self.blocks.at[target, rows],
            send_sem=self.send_sem.at[n],
            recv_sem=self.recv_sem.at[n],
            device_id={"xband": self.place[to]},
            device_id_type=MESH,
        )

    def send(self, source, target, part, n, to):
        self.copy(self.blocks.at[source] if source else self.own, target, part, n, to).start()
        self.sent.append((source, target, part, n, to))

    def wait(self, slot, part, n):
        self.copy(self.blocks.at[slot], slot, part, n, "core").wait_recv()

    def start_part(self, part):
        self.send(0, OWN[3], part, 2 + part, "long2")
        self.send(0, OWN[4], part, 4 + part, "short2")

    def start_rest(self):
        self.send(0, OWN[1], 2, 0, "long1")
        self.send(0, OWN[2], 2, 1, "short1")
        self.core(0)

    def core(self, p):
        self.send(OWN[p], OTHER[p], 2, 12 + p, "core")

    def from_core(self, p):
        self.wait(OTHER[p], 2, 12 + p)

    def run(self, compute, finish, hooks=None):
        hooks = hooks or {}
        def first():
            if "first" in hooks:
                hooks["first"]()
            for part in range(2):
                self.wait(OWN[3], part, 2 + part)
                self.send(OWN[3], OWN[5], part, 6 + part, "long1")
                self.send(OWN[3], OWN[7], part, 8 + part, "long2")
                self.wait(OWN[4], part, 4 + part)
                self.send(OWN[4], OWN[6], part, 10 + part, "short1")
                if "far" in hooks and part == 0:
                    hooks["far"]()
            self.core(3)
            self.core(4)
            for n, p in enumerate((1, 2)):
                self.wait(OWN[p], 2, n)
                self.core(p)
            self.from_core(0)

        def last():
            for p, n in ((5, 6), (6, 10), (7, 8)):
                self.wait(OWN[p], 0, n)
                self.wait(OWN[p], 1, n + 1)
                self.core(p)

        actions = {1: first, OWN[5]: last}
        for p in range(1, RING - 1):
            actions[OTHER[p]] = functools.partial(self.from_core, p)

        def one(slot, carry):
            for n, action in actions.items():
                pl.when(slot == n)(action)
                if n in hooks:
                    pl.when(slot == n)(hooks[n])
            compute(slot)
            return carry

        lax.fori_loop(0, COLUMN - 1, one, 0)
        self.from_core(RING - 1)
        finish(COLUMN - 1)

    def finish(self):
        for source, *rest in self.sent:
            self.copy(self.blocks.at[source] if source else self.own, *rest).wait_send()


def load_total(ref, q, t):
    return [ref[q, t, 8 * g : 8 * g + 8, :] for g in range(EXT // 8)]


def store_total(ref, q, t, total):
    for g, value in enumerate(total):
        ref[q, t, 8 * g : 8 * g + 8, :] = value


def kernel(
    mag_hbm, offset_hbm, shift_hbm, volume_ref, measured_ref, residual_ref, correction_ref,
    mag_ref, offset_ref, shift_ref, order,
    vols, ress, tables_vmem, tables, pair_vmem, pair_ref, seen, proj, back, other, ext, own_sums, sums,
    below, above, index_ref, weight_ref, image_0, image_1,
    vol_send, vol_recv, res_send, res_recv, slab_send, slab_recv, pair_send, pair_recv,
    values_send, values_recv, local_sem, word_sem,
):
    slab, band = lax.axis_index("zslab"), lax.axis_index("xband")
    half, core = lax.div(band, 16), lax.rem(band, 2)
    z = lax.div(lax.rem(band, 16), 2)
    turn = 1 - 2 * core
    pair = (1 - half) * COLUMN + lax.rem(band, COLUMN)

    def ring(away, core=core):
        return half * COLUMN + lax.rem(z + away + 2 * RING, RING) * 2 + core

    scalars = [
        pltpu.make_async_copy(source, target, local_sem.at[n])
        for n, (source, target) in enumerate(
            ((mag_hbm, mag_ref), (offset_hbm, offset_ref), (shift_hbm, shift_ref))
        )
    ]
    own_block = pltpu.make_async_copy(volume_ref.at[0], vols.at[0], local_sem.at[3])
    own_seen = pltpu.make_async_copy(measured_ref.at[0], seen, local_sem.at[4])
    for copy in [*scalars, own_block, own_seen]:
        copy.start()

    place = {
        "long1": ring(turn),
        "long2": ring(2 * turn),
        "short1": ring(-turn),
        "short2": ring(-2 * turn),
        "core": band + turn,
        "pair": pair,
    }
    for p, away in enumerate(AWAY):
        order[OWN[p]] = lax.rem(z - turn * away + 2 * RING, RING) * 2 + core
        order[OTHER[p]] = lax.rem(z + turn * away + 2 * RING, RING) * 2 + 1 - core
    barrier = pltpu.get_barrier_semaphore()
    for to in place.values():
        pl.semaphore_signal(barrier, inc=1, device_id={"xband": to}, device_id_type=MESH)
    slabs = [lax.rem(slab + j, SLABS) for j in range(SLABS)]
    for to in (slabs[1], slabs[SLABS - 1]):
        for of in (band, pair):
            pl.semaphore_signal(barrier, inc=1, device_id={"zslab": to, "xband": of}, device_id_type=MESH)

    pl.semaphore_wait(barrier, len(place) + 4)

    gather = Gather(vols, VOL_PARTS, vol_send, vol_recv, place, volume_ref.at[0])
    gather.start_part(0)
    gather.start_part(1)
    gather.start_rest()

    lane, row = iota(1), iota(0)
    for copy in scalars:
        copy.wait()

    def spread(angle, values):
        here = lane == angle
        mags, offsets, shifts = values
        return (
            jnp.where(here, mag_ref[angle], mags),
            jnp.where(here, offset_ref[angle].astype(jnp.float32), offsets),
            jnp.where(here, shift_ref[angle].astype(jnp.float32), shifts),
        )

    zeros = jnp.zeros((8, 128), jnp.float32)
    mags, offsets, shifts = lax.fori_loop(0, BANDS, spread, (zeros, zeros, zeros))
    tables_vmem[0] = jnp.where(row == 0, mags, jnp.where(row == 1, offsets, shifts))

    def tell(n):
        for side, to in enumerate((slabs[n + 1], slabs[SLABS - 1 - n])):
            pl.semaphore_signal(word_sem.at[n, side], inc=1, device_id={"zslab": to}, device_id_type=MESH)

    def hear(n):
        for side in range(2):
            pl.semaphore_wait(word_sem.at[n, side], 1)

    tell(0)

    def pair_copy(source, target, n):
        return pltpu.make_async_remote_copy(
            src_ref=source,
            dst_ref=target,
            send_sem=pair_send.at[n],
            recv_sem=pair_recv.at[n],
            device_id={"xband": pair},
            device_id_type=MESH,
        )

    def slab_copy(source, target, n, to, of=band):
        return pltpu.make_async_remote_copy(
            src_ref=source,
            dst_ref=target,
            send_sem=slab_send.at[n],
            recv_sem=slab_recv.at[n],
            device_id={"zslab": slabs[to], "xband": of},
            device_id_type=MESH,
        )

    pair_values = pair_copy(tables_vmem.at[0], pair_vmem, 0)
    pair_values.start()
    def values_copy(source, target, to):
        return pltpu.make_async_remote_copy(
            src_ref=tables_vmem.at[source],
            dst_ref=tables_vmem.at[target],
            send_sem=values_send.at[target],
            recv_sem=values_recv.at[target],
            device_id={"xband": place[to]},
            device_id_type=MESH,
        )

    routes = (
        (0, OWN[3], "long2"), (0, OWN[4], "short2"), (0, OWN[1], "long1"), (0, OWN[2], "short1"),
        (OWN[3], OWN[7], "long2"), (OWN[3], OWN[5], "long1"), (OWN[4], OWN[6], "short1"),
        *((OWN[p], OTHER[p], "core") for p in range(RING)),
    )
    for route in (*routes[:4], routes[7]):
        values_copy(*route).start()

    def values_on(p):
        values_copy(0, OWN[p], "core").wait_recv()
        for route in routes:
            if route[0] == OWN[p]:
                values_copy(*route).start()

    def to_smem(first, count, n):
        rows = pl.ds(first, count)
        return pltpu.make_async_copy(tables_vmem.at[rows], tables.at[rows], local_sem.at[n])

    own_table = pltpu.make_async_copy(tables_vmem.at[0], tables.at[0], local_sem.at[0])
    own_table.start()
    for t in range(TILES):
        for image in (image_0, image_1):
            image[t, 0:8, :] = zeros
            image[t, 8 + ROWS :, :] = zeros
        for q in range(2):
            proj[q, t] = jnp.zeros((EXT, 128), jnp.float32)
            back[q, t] = jnp.zeros((EXT, 128), jnp.float32)

    def fill_own(n, carry):
        angle = half * COLUMN + order[n]
        tap_tables(mag_ref[angle], offset_ref[angle].astype(jnp.float32), index_ref, weight_ref, 2 * n)
        return carry

    lax.fori_loop(0, COLUMN, fill_own, 0)

    def near_values():
        pair_values.wait_recv()
        local = pltpu.make_async_copy(pair_vmem, pair_ref, local_sem.at[1])
        local.start()
        for p in (1, 2):
            values_on(p)
        values_copy(0, OTHER[0], "core").wait_recv()
        near = to_smem(1, 5, 2)
        near.start()
        near.wait()
        local.wait()

    def core_values():
        for p in range(1, 5):
            values_copy(0, OTHER[p], "core").wait_recv()
        core = to_smem(OTHER[1], 4, 2)
        core.start()
        core.wait()

    def far_values():
        for p in (5, 6, 7):
            values_on(p)

    def last_values():
        for p in (5, 6, 7):
            values_copy(0, OTHER[p], "core").wait_recv()
        far = to_smem(OWN[5], 6, 2)
        far.start()
        far.wait()

    def fill_pair():
        def one(n, carry):
            angle = half * COLUMN + order[n]
            tap_tables(pair_ref[0, angle], pair_ref[1, angle], index_ref, weight_ref, 2 * n + 1)
            return carry

        lax.fori_loop(0, COLUMN, one, 0)

    images = (image_0, image_1)
    exchanged = []

    def start(copy):
        copy.start()
        exchanged.append(copy)

    def tiles_apart(ref, tile, phase, after):
        def finish(slot):
            for q in (1, 0):
                values = tile(slot, q)
                for t in range(TILES):
                    store_total(ref, q, t, values(t, load_total(ref, q, t)))
                    if q:
                        start(pair_copy(ref.at[1, t], other.at[phase, t], 2 + TILES * phase + t))
                of, n = (pair, 4 * phase + 2) if q else (band, 4 * phase)
                start(slab_copy(ref.at[q, :, pl.ds(ROWS, 8)], below.at[phase, q], n, 1, of))
                start(slab_copy(ref.at[q, :, pl.ds(0, 8)], above.at[phase, q], n + 1, SLABS - 1, of))
                after(q)

        return finish

    def each(ref, tile):
        def compute(slot):
            for q in range(2):
                values = tile(slot, q)
                for t in range(TILES):
                    store_total(ref, q, t, values(t, load_total(ref, q, t)))

        return compute

    def full_rows(ref, t, phase):
        for g in range(EXT // 8):
            value = ref[0, t, 8 * g : 8 * g + 8, :] + other[phase, t, 8 * g : 8 * g + 8, :]
            if g == 0:
                value = value + jnp.where(slab > 0, below[phase, 0, t] + below[phase, 1, t], 0.0)
            if g == EXT // 8 - 1:
                value = value + jnp.where(slab < SLABS - 1, above[phase, 0, t] + above[phase, 1, t], 0.0)
            ext[t, 8 * g : 8 * g + 8, :] = value

    def project(slot, q):
        angle = pair if q else band
        mag, offset, shift = (tables[slot, n, angle] for n in range(3))
        shift = jnp.clip(shift.astype(jnp.int32), -HALO, HALO)
        return lambda t, total: project_tile(vols, slot, t, mag, offset, shift, images[q], total)

    def send_sums(q):
        for t in range(TILES):
            column = jnp.zeros((1, 128), jnp.float32)
            for g in range(EXT // 8):
                value = proj[q, t, 8 * g : 8 * g + 8, :]
                if g == 0:
                    value = jnp.where(row + slab * ROWS >= HALO, value, 0.0)
                if g == EXT // 8 - 1:
                    value = jnp.where((row < HALO) | (slab < SLABS - 1), value, 0.0)
                column = column + jnp.sum(value, axis=0, keepdims=True)
            own_sums[q, t : t + 1, :] = column
        if q:
            start(pair_copy(own_sums.at[1], sums.at[SLABS], 1))
        for j in range(1, SLABS):
            start(slab_copy(own_sums.at[q], sums.at[SLABS * q + j], 7 + 7 * q + j, j, pair if q else band))

    own_seen.wait()
    for t in range(TILES):
        column = jnp.sum(seen[:, 128 * t : 128 * t + 128], axis=0, keepdims=True)
        own_sums[0, TILES + t : TILES + t + 1, :] = column
        own_sums[1, TILES + t : TILES + t + 1, :] = jnp.zeros((1, 128), jnp.float32)
    own_block.wait()
    own_table.wait()
    hooks = {
        "first": lambda: [hear(0), tell(1)],
        "far": lambda: [values_on(3), values_on(4)],
        1: near_values,
        6: core_values,
        14: lambda: hear(1),
        9: far_values,
        10: last_values,
    }
    gather.run(each(proj, project), tiles_apart(proj, project, 0, send_sums), hooks)
    fill_pair()
    for copy in exchanged:
        copy.wait_recv()

    all_sums = own_sums[0]
    for j in range(1, 2 * SLABS):
        all_sums = all_sums + sums[j]
    double = 2 * (lane & 63)
    spread_out = Gather(ress, RES_PARTS, res_send, res_recv, place)
    for t in range(TILES):
        full_rows(proj, t, 0)
        gain = all_sums[TILES + t : TILES + t + 1, :] / all_sums[t : t + 1, :]
        gain = jnp.broadcast_to(gain, (8, 128))
        for g in range(ROWS // 8):
            value = seen[8 * g : 8 * g + 8, 128 * t : 128 * t + 128]
            value = value - gain * ext[t, HALO + 8 * g : HALO + 8 * g + 8, :]
            residual_ref[0, 8 * g : 8 * g + 8, 128 * t : 128 * t + 128] = value
        if t % 2 == 0:
            continue
        k = t // 2
        for phase in range(2):
            for g in range(ROWS // 8):
                a = residual_ref[0, 8 * g : 8 * g + 8, 256 * k : 256 * k + 128]
                b = residual_ref[0, 8 * g : 8 * g + 8, 256 * k + 128 : 256 * k + 256]
                first = ROWS * (2 * k + phase) + 8 * g
                value = jnp.where(lane < 64, take(a, double + phase), take(b, double + phase))
                ress[0, first : first + 8, :] = value
        spread_out.start_part(k)
    spread_out.start_rest()

    def backproject(slot, q):
        angle = half * COLUMN + order[slot]
        shift = pair_ref[2, angle].astype(jnp.int32) if q else shift_ref[angle]
        shift = jnp.clip(shift, -HALO, HALO)
        return lambda t, total: backproject_tile(
            ress, slot, t, 2 * slot + q, shift, index_ref, weight_ref, images[q], total
        )

    before = len(exchanged)
    spread_out.run(each(back, backproject), tiles_apart(back, backproject, 1, lambda q: None))
    for copy in exchanged[before:]:
        copy.wait_recv()
    for t in range(TILES):
        full_rows(back, t, 1)
        correction_ref[0, :, 128 * t : 128 * (t + 1)] = ext[t, HALO : HALO + ROWS, :]
    gather.finish()
    spread_out.finish()
    for route in routes:
        values_copy(*route).wait_send()
    for copy in [pair_values, *exchanged]:
        copy.wait_send()


def shards(volume, measured, magnification, shift_y, shift_z):
    hbm, vmem = pl.BlockSpec(memory_space=pltpu.HBM), pl.BlockSpec(memory_space=pltpu.VMEM)
    block = jax.ShapeDtypeStruct(volume.shape, jnp.float32)
    f32 = jnp.float32
    arguments = (*(x.reshape(BANDS) for x in (magnification, shift_y, shift_z)), volume, measured)
    residual, correction = pl.pallas_call(
        kernel,
        out_shape=(block, block),
        in_specs=[hbm] * 5,
        out_specs=(vmem, vmem),
        scratch_shapes=[
            pltpu.SMEM((BANDS,), f32),
            pltpu.SMEM((BANDS,), jnp.int32),
            pltpu.SMEM((BANDS,), jnp.int32),
            pltpu.SMEM((COLUMN,), jnp.int32),
            pltpu.VMEM((COLUMN, ROWS, 128 * TILES), f32),
            pltpu.VMEM((COLUMN, RES_ROWS, 128), f32),
            pltpu.VMEM((COLUMN, 8, 128), f32),
            pltpu.SMEM((COLUMN, 8, 128), f32),
            pltpu.VMEM((8, 128), f32),
            pltpu.SMEM((8, 128), f32),
            pltpu.VMEM((ROWS, 128 * TILES), f32),
            pltpu.VMEM((2, TILES, EXT, 128), f32),
            pltpu.VMEM((2, TILES, EXT, 128), f32),
            pltpu.VMEM((2, TILES, EXT, 128), f32),
            pltpu.VMEM((TILES, EXT, 128), f32),
            pltpu.VMEM((2, 8, 128), f32),
            pltpu.VMEM((2 * SLABS, 8, 128), f32),
            pltpu.VMEM((2, 2, TILES, 8, 128), f32),
            pltpu.VMEM((2, 2, TILES, 8, 128), f32),
            pltpu.VMEM((BANDS, 128, 128), jnp.int32),
            pltpu.VMEM((BANDS, 128, 128), f32),
            pltpu.VMEM((TILES, ROWS + 16, 128), f32),
            pltpu.VMEM((TILES, ROWS + 16, 128), f32),
            pltpu.SemaphoreType.DMA((COPIES,)),
            pltpu.SemaphoreType.DMA((COPIES,)),
            pltpu.SemaphoreType.DMA((COPIES,)),
            pltpu.SemaphoreType.DMA((COPIES,)),
            pltpu.SemaphoreType.DMA((22,)),
            pltpu.SemaphoreType.DMA((22,)),
            pltpu.SemaphoreType.DMA((2 + 2 * TILES,)),
            pltpu.SemaphoreType.DMA((2 + 2 * TILES,)),
            pltpu.SemaphoreType.DMA((COLUMN,)),
            pltpu.SemaphoreType.DMA((COLUMN,)),
            pltpu.SemaphoreType.DMA((5,)),
            pltpu.SemaphoreType.REGULAR((2, 2)),
        ],
        compiler_params=pltpu.CompilerParams(
            collective_id=0, has_side_effects=True, vmem_limit_bytes=40 * 1024 * 1024
        ),
        name="sirt",
    )(*(pltpu.with_memory_space_constraint(x, pltpu.HBM) for x in arguments))
    return residual * (1.0 / BANDS), correction * (1.0 / (BANDS * math.sqrt(BANDS)))


def solution(mesh):
    return jax.shard_map(
        shards,
        mesh=mesh,
        in_specs=(
            P("xband", "zslab", None),
            P("xband", "zslab", None),
            P(None, "xband"),
            P(None, "xband"),
            P(None, "xband"),
        ),
        out_specs=(P("xband", "zslab", None), P("xband", "zslab", None)),
        check_vma=False,
    )
```
